128 devices in a mesh: dev: 128 (over x, z, y, core).
Axes of the slice: x: 4, y: 4, z: 4, core: 2. Of those that a mesh axis runs over, the one named last changes fastest.
Arguments:
- source_rows: bfloat16 [131072, 4096], P('dev'), may hold values from -6 to 6
- factor: bfloat16 [8, 512, 512], replicated, may hold values from -0.25 to 0.25
- plan_start: int32 [128, 128], replicated, may hold values from 0 to 1016, as said below
- plan_count: int32 [128, 128], replicated, may hold values from 0 to 8, as said below
- partners: int32 [2, 128], replicated, may hold values from 0 to 127, as said below
Outputs:
- kernel_tiles: float32 [2, 65536, 512], P(None, 'dev')
The draws below stay inside these ranges and needn't reach their ends.
Inputs may be any that keep to these rules, and one draw needn't show every extreme that they name: `plan_count`: entry [s, d] is how many rows source shard s sends to destination d; each column sums to exactly 512; one source's counts sum to at most 1024, and some source reaches it. `plan_start`: the row ranges of one source for the different destinations are disjoint and lie within its 1024 rows. In each round r there is one power of two m_r with partners[r, d] = d XOR m_r for every player d; the m_r of different rounds differ.
All inputs are finite; a program needn't handle non-finite values.
Results may differ from the reference program's by a relative error of at most 0.0029.
Values may be sent and summed in bfloat16 or wider, within the bound.
No kernel may reach another device: no remote copies, remote signals or barrier semaphores. Data moves between devices by JAX's collectives and lax.ppermute only.
A program may use at most 128 MiB of HBM per device.

```python
import jax
import jax.numpy as jnp
from jax import lax

BLOCK = 512
LAYERS = 8
ROWS_DEV = 512
ROUNDS = 2
FEATS = 4096
SRC_CAP = 1024
ROWS = 65536
N_DEV = 128


def plan_tables(key):
    base_key = jax.random.fold_in(key, 4242)
    key_bias, key_mix, key_force, key_split, key_order = jax.random.split(base_key, 5)
    half_count = N_DEV // 2
    slot_rows = 2 * ROWS_DEV // N_DEV
    source_bias = jax.random.randint(key_bias, (N_DEV,), 0, 4)
    forced = jax.random.randint(key_force, (), 0, N_DEV)
    source_bias = jnp.where(jnp.arange(N_DEV) == forced, 10, source_bias)
    mixing = jax.random.randint(key_mix, (N_DEV, N_DEV), 0, 2 * N_DEV)
    scores = (source_bias[:, None] * N_DEV + mixing) * N_DEV + jnp.arange(N_DEV)[:, None]
    order_rank = jnp.argsort(-scores, axis=0)
    rank_in_column = jnp.argsort(order_rank, axis=0)
    split_share = jax.random.randint(key_split, (N_DEV,), 1, slot_rows)
    counts_table = jnp.where(rank_in_column < half_count - 1, slot_rows, 0)
    counts_table = jnp.where(rank_in_column == half_count - 1, split_share[None, :], counts_table)
    counts_table = jnp.where(rank_in_column == half_count, slot_rows - split_share[None, :], counts_table)
    order_keys = jax.random.randint(key_order, (N_DEV, N_DEV), 0, 1 << 20) * N_DEV + jnp.arange(N_DEV)[None, :]
    order_dest = jnp.argsort(order_keys, axis=1)
    ordered = jnp.take_along_axis(counts_table, order_dest, axis=1)
    prefix = jnp.cumsum(ordered, axis=1) - ordered
    starts_table = jnp.take_along_axis(prefix, jnp.argsort(order_dest, axis=1), axis=1)
    return (starts_table.astype(jnp.int32), counts_table.astype(jnp.int32))


def draw_plan_start(key, part):
    return plan_tables(key)[0]


def draw_plan_count(key, part):
    return plan_tables(key)[1]


def draw_partners(key, part):
    base_key = jax.random.fold_in(key, 777)
    levels = N_DEV.bit_length() - 1
    chosen = jax.random.permutation(base_key, levels).astype(jnp.int32)
    positions = jnp.arange(N_DEV, dtype=jnp.int32)
    tables = []
    for round_index in range(ROUNDS):
        mask_value = jnp.left_shift(jnp.int32(1), chosen[round_index]).astype(jnp.int32)
        tables.append(jnp.bitwise_xor(positions, mask_value).astype(jnp.int32))
    return jnp.stack(tables).astype(jnp.int32)


def block_levels(own_key, shape, shards, least, top_value):
    factor_of = 1.0
    for axis_at, parts in shards:
        draws = jax.random.uniform(jax.random.fold_in(jax.random.fold_in(own_key, 6), axis_at), (parts,), jnp.float32, least / len(shards), top_value / len(shards))
        factor_of = factor_of * jnp.repeat(jnp.exp(draws), shape[axis_at] // parts).reshape((-1,) + (1,) * (len(shape) - 1 - axis_at))
    return factor_of


def bell_draw(own_key, shape, width, most, cuts=(), held_as=jnp.bfloat16):
    values = width * jax.random.normal(own_key, shape, jnp.float32)
    if cuts:
        values = values * block_levels(own_key, shape, cuts, -0.22, 0.18)
    return jnp.clip(values, -most, most).astype(held_as)


def setup_inputs(seed: int = 0) -> dict:
    arg_keys = jax.random.split(jax.random.key(seed), 6)
    source_rows = bell_draw(arg_keys[0], (N_DEV * SRC_CAP, FEATS), 1.0, 6.0, ((0, 128),))
    factor = bell_draw(arg_keys[1], (LAYERS, BLOCK, BLOCK), BLOCK ** -0.5, 0.25)
    plan_start = draw_plan_start(jax.random.fold_in(arg_keys[5], 71), 0)
    plan_count = draw_plan_count(jax.random.fold_in(arg_keys[5], 71), 0)
    partners = draw_partners(jax.random.fold_in(arg_keys[5], 71), 0)
    return {"source_rows": source_rows, "factor": factor, "plan_start": plan_start, "plan_count": plan_count, "partners": partners}


def precondition(row_data, factor):
    block_width = factor.shape[1]
    pieces_out = []
    for layer in range(factor.shape[0]):
        pieces_out.append(jnp.dot(row_data[:, layer * block_width:(layer + 1) * block_width], factor[layer], preferred_element_type=jnp.float32))
    return jnp.concatenate(pieces_out, axis=1).astype(jnp.bfloat16)


def balance_index(plan_start, plan_count):
    inclusive = jnp.cumsum(plan_count, axis=0).astype(jnp.int32)
    exclusive = (inclusive - plan_count).astype(jnp.int32)
    positions = jnp.arange(ROWS_DEV, dtype=jnp.int32)

    def one_destination(columns):
        running, earlier, begins = columns
        source_of = jnp.sum((running[None, :] <= positions[:, None]).astype(jnp.int32), axis=1).astype(jnp.int32)
        source_of = jnp.minimum(source_of, N_DEV - 1).astype(jnp.int32)
        return (source_of * SRC_CAP + begins[source_of] + positions - earlier[source_of]).astype(jnp.int32)

    return lax.map(one_destination, (inclusive.T, exclusive.T, plan_start.T))


def reference(source_rows, factor, plan_start, plan_count, partners):
    index_table = balance_index(plan_start, plan_count).reshape(-1).astype(jnp.int32)
    balanced = source_rows[index_table]
    conditioned = precondition(balanced, factor)
    blocks = conditioned.reshape(N_DEV, ROWS_DEV, FEATS)
    scaling = FEATS ** -0.5
    tiles = []
    for round_index in range(ROUNDS):
        pairing = partners[round_index]

        def one_tile(device):
            return jnp.dot(blocks[device], blocks[pairing[device]].T, preferred_element_type=jnp.float32) * scaling

        result = lax.map(one_tile, jnp.arange(N_DEV, dtype=jnp.int32))
        tiles.append(result.reshape(ROWS, ROWS_DEV))
    return jnp.stack(tiles)
```

```python
import functools

import jax
import jax.numpy as jnp
from jax import lax
from jax.experimental import pallas as pl
from jax.experimental.pallas import tpu as pltpu
from jax.sharding import PartitionSpec as P

SLOT = 8
LANES = 128
MEMBERS = 4


def relative_player(device, member, masks):
    player = device
    if member & 1:
        player = player ^ masks[0]
    if member & 2:
        player = player ^ masks[1]
    return player


def role_of(device, masks):
    low = jnp.where((device & masks[0]) != 0, 1, 0)
    high = jnp.where((device & masks[1]) != 0, 2, 0)
    return low + high


def pack_kernel(masks_ref, start_ref, *refs):
    sources, out_ref, wide = refs[:MEMBERS], refs[MEMBERS], refs[MEMBERS + 1]
    devices = out_ref.shape[0]
    tiles = sources[0].shape[1] // LANES
    for quarter in range(MEMBERS):
        for tile in range(tiles):
            wide[quarter * tiles + tile] = sources[quarter][:, pl.ds(tile * LANES, LANES)].astype(jnp.float32)
    masks = (masks_ref[0], masks_ref[1])

    def one_device(device, carry):
        first = role_of(device, masks) * tiles
        for member in range(MEMBERS):
            begin = start_ref[relative_player(device, member, masks)]
            for tile in range(tiles):
                rows = wide[first + tile, pl.ds(begin, SLOT), :]
                out_ref[device, pl.ds(member * SLOT, SLOT), pl.ds(tile * LANES, LANES)] = rows.astype(jnp.bfloat16)
        return carry

    lax.fori_loop(0, devices, one_device, 0, unroll=2)


def pack(source_rows, masks, start_row):
    capacity, feats = source_rows.shape
    devices = start_row.shape[0]
    quarter = feats // MEMBERS
    step = 2 * LANES
    steps = quarter // step

    def source_spec(part):
        return pl.BlockSpec((capacity, step), lambda at, *_: (0, part * steps + at))

    return pl.pallas_call(
        pack_kernel,
        grid_spec=pltpu.PrefetchScalarGridSpec(
            num_scalar_prefetch=2,
            grid=(steps,),
            in_specs=[source_spec(part) for part in range(MEMBERS)],
            out_specs=pl.BlockSpec((devices, MEMBERS * SLOT, step), lambda at, *_: (0, 0, at)),
            scratch_shapes=[pltpu.VMEM((MEMBERS * step // LANES, capacity, LANES), jnp.float32)],
        ),
        out_shape=jax.ShapeDtypeStruct((devices, MEMBERS * SLOT, quarter), jnp.bfloat16),
        compiler_params=pltpu.CompilerParams(vmem_limit_bytes=48 * 1024 * 1024),
        name="pack",
    )(masks, start_row, *([source_rows] * MEMBERS))


def partial_kernel(scale, info_ref, count_ref, received_ref, factor_ref, own_ref, lent_ref, wide, total):
    layer = pl.program_id(0)
    devices, _, width = received_ref.shape
    tiles = width // LANES
    rows = wide.shape[2] - SLOT
    masks = (info_ref[0], info_ref[1])
    players = [relative_player(info_ref[2], member, masks) for member in range(MEMBERS)]

    def one_source(source, offsets):
        later = []
        for member in range(MEMBERS):
            for tile in range(tiles):
                run = received_ref[source, pl.ds(member * SLOT, SLOT), pl.ds(tile * LANES, LANES)]
                wide[member, tile, pl.ds(offsets[member], SLOT), :] = run.astype(jnp.float32)
            later.append(offsets[member] + count_ref[source, players[member]])
        return tuple(later)

    lax.fori_loop(0, devices, one_source, (jnp.int32(0),) * MEMBERS, unroll=2)
    conditioned = []
    for member in range(MEMBERS):
        ordered = jnp.concatenate(
            [wide[member, tile, pl.ds(0, rows), :].astype(jnp.bfloat16) for tile in range(tiles)], axis=1
        )
        conditioned.append(
            jnp.dot(ordered, factor_ref[0], preferred_element_type=jnp.float32).astype(jnp.bfloat16)
        )
    for at, (left, right) in enumerate(((0, 1), (0, 2), (2, 3), (1, 3))):
        product = lax.dot_general(
            conditioned[left],
            conditioned[right],
            (((1,), (1,)), ((), ())),
            preferred_element_type=jnp.float32,
        )

        @pl.when(layer == 0)
        def _():
            total[at] = product

        @pl.when(layer != 0)
        def _():
            summed = (total[at] + product) * scale
            if at < 2:
                own_ref[at] = summed
            else:
                lent_ref[at - 2] = summed.astype(jnp.bfloat16)


def partial_tiles(received, factor, info, counts, scale):
    devices, slots, quarter = received.shape
    width = factor.shape[1]
    layers = quarter // width
    rows = devices * SLOT // 2
    assert layers == 2

    def role(info_ref):
        return role_of(info_ref[2], (info_ref[0], info_ref[1]))

    return pl.pallas_call(
        functools.partial(partial_kernel, scale),
        grid_spec=pltpu.PrefetchScalarGridSpec(
            num_scalar_prefetch=2,
            grid=(layers,),
            in_specs=[
                pl.BlockSpec((devices, slots, width), lambda at, *_: (0, 0, at)),
                pl.BlockSpec((1, width, width), lambda at, info_ref, _: (role(info_ref) * layers + at, 0, 0)),
            ],
            out_specs=[
                pl.BlockSpec((2, rows, rows), lambda at, *_: (0, 0, 0)),
                pl.BlockSpec((2, rows, rows), lambda at, *_: (0, 0, 0)),
            ],
            scratch_shapes=[
                pltpu.VMEM((MEMBERS, width // LANES, rows + SLOT, LANES), jnp.float32),
                pltpu.VMEM((MEMBERS, rows, rows), jnp.float32),
            ],
        ),
        out_shape=[
            jax.ShapeDtypeStruct((2, rows, rows), jnp.float32),
            jax.ShapeDtypeStruct((2, rows, rows), jnp.bfloat16),
        ],
        compiler_params=pltpu.CompilerParams(vmem_limit_bytes=56 * 1024 * 1024),
        name="partial_tiles",
    )(info, counts, received, factor)


def finish_kernel(order_ref, own_ref, other_ref, out_ref):
    del order_ref
    out_ref[0] = own_ref[0] + other_ref[...].astype(jnp.float32).T


def finish(order, own, other_low, other_high):
    rows = own.shape[1]

    def kernel(order_ref, own_ref, low_ref, high_ref, out_ref):
        del order_ref

        @pl.when(pl.program_id(0) == 0)
        def _():
            out_ref[0] = own_ref[0] + low_ref[...].astype(jnp.float32).T

        @pl.when(pl.program_id(0) == 1)
        def _():
            out_ref[0] = own_ref[0] + high_ref[...].astype(jnp.float32).T

    return pl.pallas_call(
        kernel,
        grid_spec=pltpu.PrefetchScalarGridSpec(
            num_scalar_prefetch=1,
            grid=(2,),
            in_specs=[
                pl.BlockSpec((1, rows, rows), lambda at, *_: (at, 0, 0)),
                pl.BlockSpec((rows, rows), lambda at, *_: (0, 0)),
                pl.BlockSpec((rows, rows), lambda at, *_: (0, 0)),
            ],
            out_specs=pl.BlockSpec((1, rows, rows), lambda at, order_ref: (order_ref[at], 0, 0)),
        ),
        out_shape=jax.ShapeDtypeStruct((2, rows, rows), jnp.float32),
        name="finish",
    )(order, own, other_low, other_high)


def exchange(pair, devices, bits, over_low, over_high):
    def branch(low, high):
        def swap(a, b):
            return (
                lax.ppermute(a, "dev", [(at, at ^ low) for at in range(devices)]),
                lax.ppermute(b, "dev", [(at, at ^ high) for at in range(devices)]),
            )

        return swap

    branches = [branch(1 << low, 1 << high) for low in range(bits) for high in range(low + 1, bits)]
    return lax.switch(pair, branches, over_low, over_high)


def per_device(source_rows, factor, plan_start, plan_count, partners):
    devices = lax.axis_size("dev")
    bits = devices.bit_length() - 1
    own_index = lax.axis_index("dev")
    round_masks = partners[:, 0]
    low, high = jnp.min(round_masks), jnp.max(round_masks)
    low_bit = sum((low >> at > 0).astype(jnp.int32) for at in range(1, bits))
    high_bit = sum((high >> at > 0).astype(jnp.int32) for at in range(1, bits))
    pair = low_bit * (2 * bits - 1 - low_bit) // 2 + high_bit - low_bit - 1
    masks = jnp.stack([low, high])
    info = jnp.stack([low, high, own_index])
    start_row = lax.dynamic_index_in_dim(plan_start, own_index, 0, keepdims=False)
    order = jnp.where(round_masks[0] < round_masks[1], jnp.arange(2), 1 - jnp.arange(2)).astype(jnp.int32)

    packed = pack(source_rows, masks, start_row)
    received = lax.all_to_all(packed, "dev", split_axis=0, concat_axis=0, tiled=True)
    own, lent = partial_tiles(received, factor, info, plan_count, source_rows.shape[1] ** -0.5)
    from_low, from_high = exchange(pair, devices, bits, lent[1], lent[0])
    half_low = own[0] + from_high.astype(jnp.float32)
    half_high = own[1] + from_low.astype(jnp.float32)
    other_low, other_high = exchange(
        pair, devices, bits, half_low.astype(jnp.bfloat16), half_high.astype(jnp.bfloat16)
    )
    return finish(order, jnp.stack([half_low, half_high]), other_low, other_high)


def solution(mesh):
    placed = (P("dev", None), P(), P(), P(), P())
    return jax.shard_map(
        per_device, mesh=mesh, in_specs=placed, out_specs=P(None, "dev", None), check_vma=False
    )
```

```python
import functools

import jax
import jax.numpy as jnp
from jax import lax
from jax.experimental import pallas as pl
from jax.experimental.pallas import tpu as pltpu
from jax.sharding import PartitionSpec as P

SLOT = 8
LANES = 128
MEMBERS = 4


def relative_player(device, member, masks):
    player = device
    if member & 1:
        player = player ^ masks[0]
    if member & 2:
        player = player ^ masks[1]
    return player


def role_of(device, masks):
    low = jnp.where((device & masks[0]) != 0, 1, 0)
    high = jnp.where((device & masks[1]) != 0, 2, 0)
    return low + high


def masks_of(partners_ref):
    first, second = partners_ref[0, 0], partners_ref[1, 0]
    return jnp.minimum(first, second), jnp.maximum(first, second)


def pack_kernel(me_ref, partners_ref, start_ref, source_ref, out_ref, pair_ref, wide, staged, sent):
    part = pl.program_id(0)
    slot = part % 2
    tiles = source_ref.shape[1] // LANES
    takers = staged.shape[1]
    low, high = masks_of(partners_ref)
    row = me_ref[0] % start_ref.shape[0]
    role_bits = jnp.where((part & 1) != 0, low, 0) | jnp.where((part & 2) != 0, high, 0)

    def drain(which):
        pltpu.make_async_copy(staged.at[which], out_ref.at[pl.ds(0, takers)], sent.at[which]).wait()

    def taker(at):
        spread = (at & (low - 1)) | ((at & ~(low - 1)) << 1)
        return (spread & (high - 1)) | ((spread & ~(high - 1)) << 1) | role_bits

    for tile in range(tiles):
        wide[tile] = source_ref[:, pl.ds(tile * LANES, LANES)].astype(jnp.float32)

    @pl.when(part == 0)
    def _():
        pair_ref[0] = pair_index(low, high, (out_ref.shape[0] - 1).bit_length())

    @pl.when(part >= 2)
    def _():
        drain(slot)

    def fill(at, carry):
        device = taker(at)
        for member in range(MEMBERS):
            begin = start_ref[row, relative_player(device, member, (low, high))]
            rows = [wide[tile, pl.ds(begin, SLOT), :] for tile in range(tiles)]
            staged[slot, at, pl.ds(member * SLOT, SLOT), :] = jnp.concatenate(rows, axis=1).astype(jnp.bfloat16)
        return carry

    def send(at, carry):
        pltpu.make_async_copy(staged.at[slot, at], out_ref.at[taker(at)], sent.at[slot]).start()
        return carry

    for half in range(2):
        begin, end = half * takers // 2, (half + 1) * takers // 2
        lax.fori_loop(begin, end, fill, 0, unroll=4)
        lax.fori_loop(begin, end, send, 0, unroll=4)

    @pl.when(part == pl.num_programs(0) - 1)
    def _():
        drain(1 - slot)
        drain(slot)


def pair_index(low, high, bits):
    low_bit = sum(jnp.where(low >= 1 << at, 1, 0) for at in range(1, bits))
    high_bit = sum(jnp.where(high >= 1 << at, 1, 0) for at in range(1, bits))
    return (low_bit * (2 * bits - 1 - low_bit)) // 2 + high_bit - low_bit - 1


def pack(source_rows, me, partners, plan_start):
    capacity, feats = source_rows.shape
    devices = plan_start.shape[0]
    quarter = feats // MEMBERS
    start_rows = 8
    return pl.pallas_call(
        pack_kernel,
        grid_spec=pltpu.PrefetchScalarGridSpec(
            num_scalar_prefetch=2,
            grid=(MEMBERS,),
            in_specs=[
                pl.BlockSpec(
                    (start_rows, devices), lambda at, me_ref, _: (me_ref[0] // start_rows, 0), memory_space=pltpu.SMEM
                ),
                pl.BlockSpec((capacity, quarter), lambda at, *_: (0, at)),
            ],
            out_specs=[
                pl.BlockSpec(memory_space=pl.ANY),
                pl.BlockSpec((1,), lambda at, *_: (0,), memory_space=pltpu.SMEM),
            ],
            scratch_shapes=[
                pltpu.VMEM((quarter // LANES, capacity, LANES), jnp.float32),
                pltpu.VMEM((2, devices // MEMBERS, MEMBERS * SLOT, quarter), jnp.bfloat16),
                pltpu.SemaphoreType.DMA((2,)),
            ],
        ),
        out_shape=[
            jax.ShapeDtypeStruct((devices, MEMBERS * SLOT, quarter), jnp.bfloat16),
            jax.ShapeDtypeStruct((1,), jnp.int32),
        ],
        compiler_params=pltpu.CompilerParams(vmem_limit_bytes=56 * 1024 * 1024),
        name="pack",
    )(me, partners, plan_start, source_rows)


def partial_kernel(scale, me_ref, partners_ref, count_ref, received_ref, factor_ref, *refs):
    own_ref, for_low_ref, for_high_ref, wide, conditioned, own_tiles, offsets, sent = refs
    step = pl.program_id(0)
    group, _, quarter = received_ref.shape
    tiles = quarter // LANES
    rows = wide.shape[2] - SLOT
    layers, width, _ = factor_ref.shape
    each = width // LANES
    masks = masks_of(partners_ref)
    players = [relative_player(me_ref[0], member, masks) for member in range(MEMBERS)]

    @pl.when(step == 0)
    def _():
        for member in range(MEMBERS):
            offsets[member] = 0

    def one_source(at, begins):
        later = []
        for member in range(MEMBERS):
            run = received_ref[at, pl.ds(member * SLOT, SLOT), :].astype(jnp.float32)
            for tile in range(tiles):
                wide[member, tile, pl.ds(begins[member], SLOT), :] = run[:, tile * LANES : (tile + 1) * LANES]
            later.append(begins[member] + count_ref[step * group + at, players[member]])
        return tuple(later)

    begins = tuple(offsets[member] for member in range(MEMBERS))
    begins = lax.fori_loop(0, group, one_source, begins, unroll=2)
    for member in range(MEMBERS):
        offsets[member] = begins[member]

    @pl.when(step == pl.num_programs(0) - 1)
    def _():
        for member in range(MEMBERS):
            for layer in range(layers):
                ordered = jnp.concatenate(
                    [
                        wide[member, layer * each + tile, pl.ds(0, rows), :].astype(jnp.bfloat16)
                        for tile in range(each)
                    ],
                    axis=1,
                )
                conditioned[member, :, pl.ds(layer * width, width)] = jnp.dot(
                    ordered, factor_ref[layer], preferred_element_type=jnp.float32
                ).astype(jnp.bfloat16)

        def tile_of(left, right):
            return scale * lax.dot_general(
                conditioned[left],
                conditioned[right],
                (((1,), (1,)), ((), ())),
                preferred_element_type=jnp.float32,
            )

        copies = [pltpu.make_async_copy(own_tiles.at[at], own_ref.at[at], sent.at[at]) for at in range(2)]
        own_tiles[0] = tile_of(0, 1)
        own_tiles[1] = tile_of(0, 2)
        copies[0].start()
        for_low_ref[...] = tile_of(1, 3).astype(jnp.bfloat16)
        copies[1].start()
        for_high_ref[...] = tile_of(2, 3).astype(jnp.bfloat16)
        copies[0].wait()
        copies[1].wait()


def partial_tiles(received, factor, me, partners, plan_count, scale):
    devices, slots, quarter = received.shape
    width = factor.shape[1]
    layers = quarter // width
    rows = devices * SLOT // 2
    group = devices // 4

    def factor_block(at, me_ref, partners_ref):
        return role_of(me_ref[0], masks_of(partners_ref)), 0, 0

    return pl.pallas_call(
        functools.partial(partial_kernel, scale),
        grid_spec=pltpu.PrefetchScalarGridSpec(
            num_scalar_prefetch=2,
            grid=(devices // group,),
            in_specs=[
                pl.BlockSpec((devices, devices), lambda at, *_: (0, 0), memory_space=pltpu.SMEM),
                pl.BlockSpec((group, slots, quarter), lambda at, *_: (at, 0, 0)),
                pl.BlockSpec((layers, width, width), factor_block),
            ],
            out_specs=[
                pl.BlockSpec(memory_space=pl.ANY),
                pl.BlockSpec((rows, rows), lambda at, *_: (0, 0)),
                pl.BlockSpec((rows, rows), lambda at, *_: (0, 0)),
            ],
            scratch_shapes=[
                pltpu.VMEM((MEMBERS, quarter // LANES, rows + SLOT, LANES), jnp.float32),
                pltpu.VMEM((MEMBERS, rows, quarter), jnp.bfloat16),
                pltpu.VMEM((2, rows, rows), jnp.float32),
                pltpu.SMEM((MEMBERS,), jnp.int32),
                pltpu.SemaphoreType.DMA((2,)),
            ],
        ),
        out_shape=[
            jax.ShapeDtypeStruct((2, rows, rows), jnp.float32),
            jax.ShapeDtypeStruct((rows, rows), jnp.bfloat16),
            jax.ShapeDtypeStruct((rows, rows), jnp.bfloat16),
        ],
        compiler_params=pltpu.CompilerParams(vmem_limit_bytes=56 * 1024 * 1024),
        name="partial_tiles",
    )(me, partners, plan_count, received, factor)


def half_sums_kernel(own_ref, first_ref, second_ref, *out_refs):
    for at, (added_ref, out_ref) in enumerate(zip((first_ref, second_ref), out_refs)):

        @pl.when(pl.program_id(0) == at)
        def _():
            out_ref[...] = (own_ref[0] + added_ref[...].astype(jnp.float32)).astype(jnp.bfloat16)


def half_sums(own, first, second):
    rows = own.shape[1]
    whole = pl.BlockSpec((rows, rows), lambda at: (0, 0))
    return pl.pallas_call(
        half_sums_kernel,
        grid=(2,),
        in_specs=[pl.BlockSpec((1, rows, rows), lambda at: (at, 0, 0)), whole, whole],
        out_specs=[whole, whole],
        out_shape=[jax.ShapeDtypeStruct((rows, rows), jnp.bfloat16)] * 2,
        name="half_sums",
    )(own, first, second)


def finish_kernel(partners_ref, own_ref, *refs):
    added, turned, out_ref = refs[:2], refs[2:4], refs[4]
    for at in range(2):

        @pl.when(pl.program_id(0) == at)
        def _():
            out_ref[0] = (
                own_ref[0] + added[at][...].astype(jnp.float32) + turned[at][...].astype(jnp.float32).T
            )


def finish(partners, own, added, turned):
    rows = own.shape[1]

    def out_block(at, partners_ref):
        swapped = jnp.where(partners_ref[0, 0] < partners_ref[1, 0], 0, 1)
        return at ^ swapped, 0, 0

    return pl.pallas_call(
        finish_kernel,
        grid_spec=pltpu.PrefetchScalarGridSpec(
            num_scalar_prefetch=1,
            grid=(2,),
            in_specs=[
                pl.BlockSpec((1, rows, rows), lambda at, *_: (at, 0, 0)),
                *[pl.BlockSpec((rows, rows), lambda at, *_: (0, 0))] * 4,
            ],
            out_specs=pl.BlockSpec((1, rows, rows), out_block),
        ),
        out_shape=jax.ShapeDtypeStruct((2, rows, rows), jnp.float32),
        name="finish",
    )(partners, own, *added, *turned)


def exchange(pair, devices, bits, over_low, over_high):
    def branch(low, high):
        def swap(a, b):
            return (
                lax.ppermute(a, "dev", [(at, at ^ low) for at in range(devices)]),
                lax.ppermute(b, "dev", [(at, at ^ high) for at in range(devices)]),
            )

        return swap

    branches = [branch(1 << low, 1 << high) for low in range(bits) for high in range(low + 1, bits)]
    return lax.switch(pair, branches, over_low, over_high)


def per_device(source_rows, factor, plan_start, plan_count, partners):
    devices = lax.axis_size("dev")
    bits = devices.bit_length() - 1
    me = lax.axis_index("dev").reshape(1)
    packed, pair = pack(source_rows, me, partners, plan_start)
    received = lax.all_to_all(packed, "dev", split_axis=0, concat_axis=0, tiled=True)
    received, pair = lax.optimization_barrier((received, pair))
    own, for_low, for_high = partial_tiles(received, factor, me, partners, plan_count, source_rows.shape[1] ** -0.5)
    from_low, from_high = exchange(pair[0], devices, bits, for_low, for_high)
    halves = half_sums(own, from_high, from_low)
    return finish(partners, own, (from_high, from_low), exchange(pair[0], devices, bits, *halves))


def solution(mesh):
    placed = (P("dev", None), P(), P(), P(), P())
    return jax.shard_map(
        per_device, mesh=mesh, in_specs=placed, out_specs=P(None, "dev", None), check_vma=False
    )
```

```python
import functools

import jax
import jax.numpy as jnp
from jax import lax
from jax.experimental import pallas as pl
from jax.experimental.pallas import tpu as pltpu
from jax.sharding import PartitionSpec as P

SLOT = 8
LANES = 128
MEMBERS = 4


def relative_player(device, member, masks):
    player = device
    if member & 1:
        player = player ^ masks[0]
    if member & 2:
        player = player ^ masks[1]
    return player


def role_of(device, masks):
    low = jnp.where((device & masks[0]) != 0, 1, 0)
    high = jnp.where((device & masks[1]) != 0, 2, 0)
    return low + high


def masks_of(partners_ref):
    first, second = partners_ref[0, 0], partners_ref[1, 0]
    return jnp.minimum(first, second), jnp.maximum(first, second)


def pack_kernel(me_ref, partners_ref, start_hbm, source_hbm, out_hbm, pair_ref, *scratch):
    source, wide, staged, start, got, sent, start_got = scratch
    parts, capacity, quarter = source.shape
    tiles = quarter // LANES
    takers = staged.shape[1]
    start_rows = start.shape[0]
    low, high = masks_of(partners_ref)
    row = me_ref[0] % start_rows

    def load(part):
        return pltpu.make_async_copy(
            source_hbm.at[:, pl.ds(part * quarter, quarter)], source.at[part], got.at[part]
        )

    start_load = pltpu.make_async_copy(
        start_hbm.at[pl.ds(pl.multiple_of(me_ref[0] - row, start_rows), start_rows)], start, start_got
    )
    start_load.start()
    for part in range(parts):
        load(part).start()
    pair_ref[0] = pair_index(low, high, (out_hbm.shape[0] - 1).bit_length())
    start_load.wait()

    def one_part(part, carry):
        role_bits = jnp.where((part & 1) != 0, low, 0) | jnp.where((part & 2) != 0, high, 0)

        def taker(at):
            spread = (at & (low - 1)) | ((at & ~(low - 1)) << 1)
            return (spread & (high - 1)) | ((spread & ~(high - 1)) << 1) | role_bits

        def fill(at, carry):
            device = taker(at)
            for member in range(MEMBERS):
                begin = start[row, relative_player(device, member, (low, high))]
                rows = [wide[tile, pl.ds(begin, SLOT), :] for tile in range(tiles)]
                staged[part, at, pl.ds(member * SLOT, SLOT), :] = jnp.concatenate(rows, axis=1).astype(jnp.bfloat16)
            return carry

        def send(at, carry):
            pltpu.make_async_copy(staged.at[part, at], out_hbm.at[taker(at)], sent.at[part]).start()
            return carry

        load(part).wait()
        for tile in range(tiles):
            wide[tile] = source[part, :, pl.ds(tile * LANES, LANES)].astype(jnp.float32)
        for half in range(2):
            begin, end = half * takers // 2, (half + 1) * takers // 2
            lax.fori_loop(begin, end, fill, 0, unroll=4)
            lax.fori_loop(begin, end, send, 0, unroll=4)
        return carry

    lax.fori_loop(0, parts, one_part, 0)
    for part in range(parts):
        pltpu.make_async_copy(staged.at[part], out_hbm.at[pl.ds(0, takers)], sent.at[part]).wait()


def pair_index(low, high, bits):
    low_bit = sum(jnp.where(low >= 1 << at, 1, 0) for at in range(1, bits))
    high_bit = sum(jnp.where(high >= 1 << at, 1, 0) for at in range(1, bits))
    return (low_bit * (2 * bits - 1 - low_bit)) // 2 + high_bit - low_bit - 1


def pack(source_rows, me, partners, plan_start):
    capacity, feats = source_rows.shape
    devices = plan_start.shape[0]
    quarter = feats // MEMBERS
    smem, anywhere = pl.BlockSpec(memory_space=pltpu.SMEM), pl.BlockSpec(memory_space=pl.ANY)
    return pl.pallas_call(
        pack_kernel,
        in_specs=[smem, smem, anywhere, anywhere],
        out_specs=[anywhere, smem],
        scratch_shapes=[
            pltpu.VMEM((MEMBERS, capacity, quarter), jnp.bfloat16),
            pltpu.VMEM((quarter // LANES, capacity, LANES), jnp.float32),
            pltpu.VMEM((MEMBERS, devices // MEMBERS, MEMBERS * SLOT, quarter), jnp.bfloat16),
            pltpu.SMEM((8, devices), jnp.int32),
            pltpu.SemaphoreType.DMA((MEMBERS,)),
            pltpu.SemaphoreType.DMA((MEMBERS,)),
            pltpu.SemaphoreType.DMA,
        ],
        out_shape=[
            jax.ShapeDtypeStruct((devices, MEMBERS * SLOT, quarter), jnp.bfloat16),
            jax.ShapeDtypeStruct((1,), jnp.int32),
        ],
        compiler_params=pltpu.CompilerParams(vmem_limit_bytes=56 * 1024 * 1024),
        name="pack",
    )(me, partners, plan_start, source_rows)


def partial_kernel(scale, me_ref, partners_ref, count_hbm, received_hbm, factor_hbm, *refs):
    out_hbm, (received, factor, wide, conditioned, own, lent, count, got, loaded, sent) = refs[:3], refs[3:]
    groups, group, _, quarter = received.shape
    tiles = quarter // LANES
    rows = wide.shape[2] - SLOT
    layers, width, _ = factor.shape
    each = width // LANES
    masks = masks_of(partners_ref)
    players = [relative_player(me_ref[0], member, masks) for member in range(MEMBERS)]

    def load(at):
        return pltpu.make_async_copy(received_hbm.at[pl.ds(at * group, group)], received.at[at], got.at[at])

    count_load = pltpu.make_async_copy(count_hbm, count, loaded.at[0])
    factor_load = pltpu.make_async_copy(
        factor_hbm.at[pl.ds(role_of(me_ref[0], masks) * layers, layers)], factor, loaded.at[1]
    )
    count_load.start()
    for at in range(groups):
        load(at).start()
    factor_load.start()
    count_load.wait()

    def one_group(at, begins):
        def one_source(source, begins):
            later = []
            for member in range(MEMBERS):
                run = received[at, source, pl.ds(member * SLOT, SLOT), :].astype(jnp.float32)
                for tile in range(tiles):
                    wide[member, tile, pl.ds(begins[member], SLOT), :] = run[:, tile * LANES : (tile + 1) * LANES]
                later.append(begins[member] + count[at * group + source, players[member]])
            return tuple(later)

        load(at).wait()
        return lax.fori_loop(0, group, one_source, begins, unroll=4)

    lax.fori_loop(0, groups, one_group, (jnp.int32(0),) * MEMBERS)
    factor_load.wait()
    for member in range(MEMBERS):
        for layer in range(layers):
            ordered = jnp.concatenate(
                [
                    wide[member, layer * each + tile, pl.ds(0, rows), :].astype(jnp.bfloat16)
                    for tile in range(each)
                ],
                axis=1,
            )
            conditioned[member, :, pl.ds(layer * width, width)] = jnp.dot(
                ordered, factor[layer], preferred_element_type=jnp.float32
            ).astype(jnp.bfloat16)

    def tile_of(left, right):
        return scale * lax.dot_general(
            conditioned[left],
            conditioned[right],
            (((1,), (1,)), ((), ())),
            preferred_element_type=jnp.float32,
        )

    copies = [
        pltpu.make_async_copy(own, out_hbm[0], sent.at[0]),
        pltpu.make_async_copy(lent.at[0], out_hbm[1], sent.at[1]),
        pltpu.make_async_copy(lent.at[1], out_hbm[2], sent.at[2]),
    ]
    own[0] = tile_of(0, 1)
    own[1] = tile_of(0, 2)
    lent[0] = tile_of(1, 3).astype(jnp.bfloat16)
    copies[0].start()
    lent[1] = tile_of(2, 3).astype(jnp.bfloat16)
    copies[1].start()
    copies[2].start()
    for copy in copies:
        copy.wait()


def partial_tiles(received, factor, me, partners, plan_count, scale):
    devices, slots, quarter = received.shape
    width = factor.shape[1]
    layers = quarter // width
    rows = devices * SLOT // 2
    groups = 8
    smem, anywhere = pl.BlockSpec(memory_space=pltpu.SMEM), pl.BlockSpec(memory_space=pl.ANY)
    return pl.pallas_call(
        functools.partial(partial_kernel, scale),
        in_specs=[smem, smem, anywhere, anywhere, anywhere],
        out_specs=[anywhere, anywhere, anywhere],
        scratch_shapes=[
            pltpu.VMEM((groups, devices // groups, slots, quarter), jnp.bfloat16),
            pltpu.VMEM((layers, width, width), jnp.bfloat16),
            pltpu.VMEM((MEMBERS, quarter // LANES, rows + SLOT, LANES), jnp.float32),
            pltpu.VMEM((MEMBERS, rows, quarter), jnp.bfloat16),
            pltpu.VMEM((2, rows, rows), jnp.float32),
            pltpu.VMEM((2, rows, rows), jnp.bfloat16),
            pltpu.SMEM((devices, devices), jnp.int32),
            pltpu.SemaphoreType.DMA((groups,)),
            pltpu.SemaphoreType.DMA((2,)),
            pltpu.SemaphoreType.DMA((3,)),
        ],
        out_shape=[
            jax.ShapeDtypeStruct((2, rows, rows), jnp.float32),
            jax.ShapeDtypeStruct((rows, rows), jnp.bfloat16),
            jax.ShapeDtypeStruct((rows, rows), jnp.bfloat16),
        ],
        compiler_params=pltpu.CompilerParams(vmem_limit_bytes=56 * 1024 * 1024),
        name="partial_tiles",
    )(me, partners, plan_count, received, factor)


def half_sums_kernel(own_hbm, *refs):
    added_hbm, out_hbm, (own, added, half, got, sent) = refs[:2], refs[2:4], refs[4:]
    loads = [
        [
            pltpu.make_async_copy(own_hbm.at[at], own.at[at], got.at[2 * at]),
            pltpu.make_async_copy(added_hbm[at], added.at[at], got.at[2 * at + 1]),
        ]
        for at in range(2)
    ]
    sends = [pltpu.make_async_copy(half.at[at], out_hbm[at], sent.at[at]) for at in range(2)]
    for load in loads[0] + loads[1]:
        load.start()
    for at in range(2):
        for load in loads[at]:
            load.wait()
        half[at] = (own[at] + added[at].astype(jnp.float32)).astype(jnp.bfloat16)
        sends[at].start()
    for send in sends:
        send.wait()


def half_sums(own, first, second):
    rows = own.shape[1]
    anywhere = pl.BlockSpec(memory_space=pl.ANY)
    return pl.pallas_call(
        half_sums_kernel,
        in_specs=[anywhere] * 3,
        out_specs=[anywhere] * 2,
        scratch_shapes=[
            pltpu.VMEM((2, rows, rows), jnp.float32),
            pltpu.VMEM((2, rows, rows), jnp.bfloat16),
            pltpu.VMEM((2, rows, rows), jnp.bfloat16),
            pltpu.SemaphoreType.DMA((4,)),
            pltpu.SemaphoreType.DMA((2,)),
        ],
        out_shape=[jax.ShapeDtypeStruct((rows, rows), jnp.bfloat16)] * 2,
        name="half_sums",
    )(own, first, second)


def finish_kernel(partners_ref, own_hbm, *refs):
    added_hbm, turned_hbm, out_hbm, (own, added, turned, tile, got, sent) = refs[:2], refs[2:4], refs[4], refs[5:]
    swapped = jnp.where(partners_ref[0, 0] < partners_ref[1, 0], 0, 1)
    loads = [
        [
            pltpu.make_async_copy(own_hbm.at[at], own.at[at], got.at[3 * at]),
            pltpu.make_async_copy(added_hbm[at], added.at[at], got.at[3 * at + 1]),
            pltpu.make_async_copy(turned_hbm[at], turned.at[at], got.at[3 * at + 2]),
        ]
        for at in range(2)
    ]
    sends = [pltpu.make_async_copy(tile.at[at], out_hbm.at[at ^ swapped], sent.at[at]) for at in range(2)]
    for load in loads[0] + loads[1]:
        load.start()
    for at in range(2):
        for load in loads[at]:
            load.wait()
        tile[at] = own[at] + added[at].astype(jnp.float32) + turned[at].astype(jnp.float32).T
        sends[at].start()
    for send in sends:
        send.wait()


def finish(partners, own, added, turned):
    rows = own.shape[1]
    smem, anywhere = pl.BlockSpec(memory_space=pltpu.SMEM), pl.BlockSpec(memory_space=pl.ANY)
    return pl.pallas_call(
        finish_kernel,
        in_specs=[smem, *[anywhere] * 5],
        out_specs=anywhere,
        scratch_shapes=[
            pltpu.VMEM((2, rows, rows), jnp.float32),
            pltpu.VMEM((2, rows, rows), jnp.bfloat16),
            pltpu.VMEM((2, rows, rows), jnp.bfloat16),
            pltpu.VMEM((2, rows, rows), jnp.float32),
            pltpu.SemaphoreType.DMA((6,)),
            pltpu.SemaphoreType.DMA((2,)),
        ],
        out_shape=jax.ShapeDtypeStruct((2, rows, rows), jnp.float32),
        name="finish",
    )(partners, own, *added, *turned)


def exchange(pair, devices, bits, over_low, over_high):
    def branch(low, high):
        def swap(a, b):
            return (
                lax.ppermute(a, "dev", [(at, at ^ low) for at in range(devices)]),
                lax.ppermute(b, "dev", [(at, at ^ high) for at in range(devices)]),
            )

        return swap

    branches = [branch(1 << low, 1 << high) for low in range(bits) for high in range(low + 1, bits)]
    return lax.switch(pair, branches, over_low, over_high)


def per_device(source_rows, factor, plan_start, plan_count, partners):
    devices = lax.axis_size("dev")
    bits = devices.bit_length() - 1
    me = lax.axis_index("dev").reshape(1)
    packed, pair = pack(source_rows, me, partners, plan_start)
    received = lax.all_to_all(packed, "dev", split_axis=0, concat_axis=0, tiled=True)
    received, pair = lax.optimization_barrier((received, pair))
    own, for_low, for_high = partial_tiles(received, factor, me, partners, plan_count, source_rows.shape[1] ** -0.5)
    from_low, from_high = exchange(pair[0], devices, bits, for_low, for_high)
    halves = half_sums(own, from_high, from_low)
    return finish(partners, own, (from_high, from_low), exchange(pair[0], devices, bits, *halves))


def solution(mesh):
    placed = (P("dev", None), P(), P(), P(), P())
    return jax.shard_map(
        per_device, mesh=mesh, in_specs=placed, out_specs=P(None, "dev", None), check_vma=False
    )
```

```python
import functools

import jax
import jax.numpy as jnp
from jax import lax
from jax.experimental import pallas as pl
from jax.experimental.pallas import tpu as pltpu
from jax.sharding import PartitionSpec as P

SLOT = 8
LANES = 128
MEMBERS = 4


def relative_player(device, member, masks):
    player = device
    if member & 1:
        player = player ^ masks[0]
    if member & 2:
        player = player ^ masks[1]
    return player


def role_of(device, masks):
    low = jnp.where((device & masks[0]) != 0, 1, 0)
    high = jnp.where((device & masks[1]) != 0, 2, 0)
    return low + high


def masks_of(partners_ref):
    first, second = partners_ref[0, 0], partners_ref[1, 0]
    return jnp.minimum(first, second), jnp.maximum(first, second)


def pack_kernel(me_ref, partners_ref, start_hbm, source_hbm, out_hbm, pair_ref, *scratch):
    source, wide, staged, start, got, sent, start_got = scratch
    parts, capacity, quarter = source.shape
    tiles = quarter // LANES
    takers = staged.shape[1]
    start_rows = start.shape[0]
    low, high = masks_of(partners_ref)
    row = me_ref[0] % start_rows

    def load(part):
        return pltpu.make_async_copy(
            source_hbm.at[:, pl.ds(part * quarter, quarter)], source.at[part], got.at[part]
        )

    start_load = pltpu.make_async_copy(
        start_hbm.at[pl.ds(pl.multiple_of(me_ref[0] - row, start_rows), start_rows)], start, start_got
    )
    start_load.start()
    for part in range(parts):
        load(part).start()
    pair_ref[0] = pair_index(low, high, (out_hbm.shape[0] - 1).bit_length())
    start_load.wait()

    def one_part(part, carry):
        role_bits = jnp.where((part & 1) != 0, low, 0) | jnp.where((part & 2) != 0, high, 0)

        def taker(at):
            spread = (at & (low - 1)) | ((at & ~(low - 1)) << 1)
            return (spread & (high - 1)) | ((spread & ~(high - 1)) << 1) | role_bits

        def fill(at, carry):
            device = taker(at)
            for member in range(MEMBERS):
                begin = start[row, relative_player(device, member, (low, high))]
                rows = [wide[tile, pl.ds(begin, SLOT), :] for tile in range(tiles)]
                staged[part, at, pl.ds(member * SLOT, SLOT), :] = jnp.concatenate(rows, axis=1).astype(jnp.bfloat16)
            return carry

        def send(at, carry):
            pltpu.make_async_copy(staged.at[part, at], out_hbm.at[taker(at)], sent.at[part]).start()
            return carry

        load(part).wait()
        for tile in range(tiles):
            wide[tile] = source[part, :, pl.ds(tile * LANES, LANES)].astype(jnp.float32)
        for half in range(2):
            begin, end = half * takers // 2, (half + 1) * takers // 2
            lax.fori_loop(begin, end, fill, 0, unroll=4)
            lax.fori_loop(begin, end, send, 0, unroll=4)
        return carry

    lax.fori_loop(0, parts, one_part, 0)
    for part in range(parts):
        pltpu.make_async_copy(staged.at[part], out_hbm.at[pl.ds(0, takers)], sent.at[part]).wait()


def pair_index(low, high, bits):
    low_bit = sum(jnp.where(low >= 1 << at, 1, 0) for at in range(1, bits))
    high_bit = sum(jnp.where(high >= 1 << at, 1, 0) for at in range(1, bits))
    return (low_bit * (2 * bits - 1 - low_bit)) // 2 + high_bit - low_bit - 1


def pack(source_rows, me, partners, plan_start):
    capacity, feats = source_rows.shape
    devices = plan_start.shape[0]
    quarter = feats // MEMBERS
    smem, anywhere = pl.BlockSpec(memory_space=pltpu.SMEM), pl.BlockSpec(memory_space=pl.ANY)
    return pl.pallas_call(
        pack_kernel,
        in_specs=[smem, smem, anywhere, anywhere],
        out_specs=[anywhere, smem],
        scratch_shapes=[
            pltpu.VMEM((MEMBERS, capacity, quarter), jnp.bfloat16),
            pltpu.VMEM((quarter // LANES, capacity, LANES), jnp.float32),
            pltpu.VMEM((MEMBERS, devices // MEMBERS, MEMBERS * SLOT, quarter), jnp.bfloat16),
            pltpu.SMEM((8, devices), jnp.int32),
            pltpu.SemaphoreType.DMA((MEMBERS,)),
            pltpu.SemaphoreType.DMA((MEMBERS,)),
            pltpu.SemaphoreType.DMA,
        ],
        out_shape=[
            jax.ShapeDtypeStruct((devices, MEMBERS * SLOT, quarter), jnp.bfloat16),
            jax.ShapeDtypeStruct((1,), jnp.int32),
        ],
        compiler_params=pltpu.CompilerParams(vmem_limit_bytes=56 * 1024 * 1024),
        name="pack",
    )(me, partners, plan_start, source_rows)


def partial_kernel(scale, me_ref, partners_ref, count_hbm, received_hbm, factor_hbm, *refs):
    own, *out_hbm = refs[:3]
    received, factor, wide, conditioned, lent, count, got, loaded, sent = refs[3:]
    groups, group, _, quarter = received.shape
    tiles = quarter // LANES
    rows = wide.shape[2] - SLOT
    layers, width, _ = factor.shape
    each = width // LANES
    masks = masks_of(partners_ref)
    players = [relative_player(me_ref[0], member, masks) for member in range(MEMBERS)]

    def load(at):
        return pltpu.make_async_copy(received_hbm.at[pl.ds(at * group, group)], received.at[at], got.at[at])

    count_load = pltpu.make_async_copy(count_hbm, count, loaded.at[0])
    factor_load = pltpu.make_async_copy(
        factor_hbm.at[pl.ds(role_of(me_ref[0], masks) * layers, layers)], factor, loaded.at[1]
    )
    count_load.start()
    for at in range(groups):
        load(at).start()
    factor_load.start()
    count_load.wait()

    def one_group(at, begins):
        def one_source(source, begins):
            later = []
            for member in range(MEMBERS):
                run = received[at, source, pl.ds(member * SLOT, SLOT), :].astype(jnp.float32)
                for tile in range(tiles):
                    wide[member, tile, pl.ds(begins[member], SLOT), :] = run[:, tile * LANES : (tile + 1) * LANES]
                later.append(begins[member] + count[at * group + source, players[member]])
            return tuple(later)

        load(at).wait()
        return lax.fori_loop(0, group, one_source, begins, unroll=4)

    lax.fori_loop(0, groups, one_group, (jnp.int32(0),) * MEMBERS)
    factor_load.wait()
    for member in range(MEMBERS):
        for layer in range(layers):
            ordered = jnp.concatenate(
                [
                    wide[member, layer * each + tile, pl.ds(0, rows), :].astype(jnp.bfloat16)
                    for tile in range(each)
                ],
                axis=1,
            )
            conditioned[member, :, pl.ds(layer * width, width)] = jnp.dot(
                ordered, factor[layer], preferred_element_type=jnp.float32
            ).astype(jnp.bfloat16)

    def tile_of(left, right):
        return scale * lax.dot_general(
            conditioned[left],
            conditioned[right],
            (((1,), (1,)), ((), ())),
            preferred_element_type=jnp.float32,
        )

    copies = [pltpu.make_async_copy(lent.at[at], out_hbm[at], sent.at[at]) for at in range(2)]
    lent[0] = tile_of(1, 3).astype(jnp.bfloat16)
    lent[1] = tile_of(2, 3).astype(jnp.bfloat16)
    copies[0].start()
    own[0] = tile_of(0, 1)
    copies[1].start()
    own[1] = tile_of(0, 2)
    for copy in copies:
        copy.wait()


def partial_tiles(received, factor, me, partners, plan_count, scale):
    devices, slots, quarter = received.shape
    width = factor.shape[1]
    layers = quarter // width
    rows = devices * SLOT // 2
    groups = 8
    smem, anywhere = pl.BlockSpec(memory_space=pltpu.SMEM), pl.BlockSpec(memory_space=pl.ANY)
    return pl.pallas_call(
        functools.partial(partial_kernel, scale),
        in_specs=[smem, smem, anywhere, anywhere, anywhere],
        out_specs=[pl.BlockSpec(memory_space=pltpu.VMEM), anywhere, anywhere],
        scratch_shapes=[
            pltpu.VMEM((groups, devices // groups, slots, quarter), jnp.bfloat16),
            pltpu.VMEM((layers, width, width), jnp.bfloat16),
            pltpu.VMEM((MEMBERS, quarter // LANES, rows + SLOT, LANES), jnp.float32),
            pltpu.VMEM((MEMBERS, rows, quarter), jnp.bfloat16),
            pltpu.VMEM((2, rows, rows), jnp.bfloat16),
            pltpu.SMEM((devices, devices), jnp.int32),
            pltpu.SemaphoreType.DMA((groups,)),
            pltpu.SemaphoreType.DMA((2,)),
            pltpu.SemaphoreType.DMA((2,)),
        ],
        out_shape=[
            pltpu.VMEM((2, rows, rows), jnp.float32),
            jax.ShapeDtypeStruct((rows, rows), jnp.bfloat16),
            jax.ShapeDtypeStruct((rows, rows), jnp.bfloat16),
        ],
        compiler_params=pltpu.CompilerParams(vmem_limit_bytes=40 * 1024 * 1024),
        name="partial_tiles",
    )(me, partners, plan_count, received, factor)


def half_sums_kernel(own, *refs):
    added_hbm, out_hbm, (added, half, got, sent) = refs[:2], refs[2:4], refs[4:]
    loads = [pltpu.make_async_copy(added_hbm[at], added.at[at], got.at[at]) for at in range(2)]
    sends = [pltpu.make_async_copy(half.at[at], out_hbm[at], sent.at[at]) for at in range(2)]
    for load in loads:
        load.start()
    for at in range(2):
        loads[at].wait()
        half[at] = (own[at] + added[at].astype(jnp.float32)).astype(jnp.bfloat16)
        sends[at].start()
    for send in sends:
        send.wait()


def half_sums(own, first, second):
    rows = own.shape[1]
    anywhere, vmem = pl.BlockSpec(memory_space=pl.ANY), pl.BlockSpec(memory_space=pltpu.VMEM)
    return pl.pallas_call(
        half_sums_kernel,
        in_specs=[vmem, anywhere, anywhere],
        out_specs=[anywhere, anywhere],
        scratch_shapes=[
            pltpu.VMEM((2, rows, rows), jnp.bfloat16),
            pltpu.VMEM((2, rows, rows), jnp.bfloat16),
            pltpu.SemaphoreType.DMA((2,)),
            pltpu.SemaphoreType.DMA((2,)),
        ],
        out_shape=[jax.ShapeDtypeStruct((rows, rows), jnp.bfloat16)] * 2,
        compiler_params=pltpu.CompilerParams(vmem_limit_bytes=16 * 1024 * 1024),
        name="half_sums",
    )(pltpu.with_memory_space_constraint(own, pltpu.VMEM), first, second)


def finish_kernel(partners_ref, own, *refs):
    added_hbm, turned_hbm, out_hbm, (added, turned, tile, got, sent) = refs[:2], refs[2:4], refs[4], refs[5:]
    swapped = jnp.where(partners_ref[0, 0] < partners_ref[1, 0], 0, 1)
    loads = [
        [
            pltpu.make_async_copy(added_hbm[at], added.at[at], got.at[2 * at]),
            pltpu.make_async_copy(turned_hbm[at], turned.at[at], got.at[2 * at + 1]),
        ]
        for at in range(2)
    ]
    sends = [pltpu.make_async_copy(tile.at[at], out_hbm.at[at ^ swapped], sent.at[at]) for at in range(2)]
    for load in loads[0] + loads[1]:
        load.start()
    for at in range(2):
        for load in loads[at]:
            load.wait()
        tile[at] = own[at] + added[at].astype(jnp.float32) + turned[at].astype(jnp.float32).T
        sends[at].start()
    for send in sends:
        send.wait()


def finish(partners, own, added, turned):
    rows = own.shape[1]
    smem, anywhere = pl.BlockSpec(memory_space=pltpu.SMEM), pl.BlockSpec(memory_space=pl.ANY)
    return pl.pallas_call(
        finish_kernel,
        in_specs=[smem, pl.BlockSpec(memory_space=pltpu.VMEM), *[anywhere] * 4],
        out_specs=anywhere,
        scratch_shapes=[
            pltpu.VMEM((2, rows, rows), jnp.bfloat16),
            pltpu.VMEM((2, rows, rows), jnp.bfloat16),
            pltpu.VMEM((2, rows, rows), jnp.float32),
            pltpu.SemaphoreType.DMA((4,)),
            pltpu.SemaphoreType.DMA((2,)),
        ],
        out_shape=jax.ShapeDtypeStruct((2, rows, rows), jnp.float32),
        compiler_params=pltpu.CompilerParams(vmem_limit_bytes=16 * 1024 * 1024),
        name="finish",
    )(partners, pltpu.with_memory_space_constraint(own, pltpu.VMEM), *added, *turned)


def exchange(pair, devices, bits, over_low, over_high):
    def branch(low, high):
        def swap(a, b):
            return (
                lax.ppermute(a, "dev", [(at, at ^ low) for at in range(devices)]),
                lax.ppermute(b, "dev", [(at, at ^ high) for at in range(devices)]),
            )

        return swap

    branches = [branch(1 << low, 1 << high) for low in range(bits) for high in range(low + 1, bits)]
    return lax.switch(pair, branches, over_low, over_high)


def per_device(source_rows, factor, plan_start, plan_count, partners):
    devices = lax.axis_size("dev")
    bits = devices.bit_length() - 1
    me = lax.axis_index("dev").reshape(1)
    packed, pair = pack(source_rows, me, partners, plan_start)
    received = lax.all_to_all(packed, "dev", split_axis=0, concat_axis=0, tiled=True)
    received, pair = lax.optimization_barrier((received, pair))
    own, for_low, for_high = partial_tiles(received, factor, me, partners, plan_count, source_rows.shape[1] ** -0.5)
    from_low, from_high = exchange(pair[0], devices, bits, for_low, for_high)
    halves = half_sums(own, from_high, from_low)
    return finish(partners, own, (from_high, from_low), exchange(pair[0], devices, bits, *halves))


def solution(mesh):
    placed = (P("dev", None), P(), P(), P(), P())
    return jax.shard_map(
        per_device, mesh=mesh, in_specs=placed, out_specs=P(None, "dev", None), check_vma=False
    )
```

```python
import functools

import jax
import jax.numpy as jnp
from jax import lax
from jax.experimental import pallas as pl
from jax.experimental.pallas import tpu as pltpu
from jax.sharding import PartitionSpec as P

SLOT = 8
LANES = 128
MEMBERS = 4
RING_BITS = 0b0101010


def shares_ring(low, high):
    return ((low & RING_BITS) != 0) & (high == 2 * low)


def relative_player(device, member, masks):
    player = device
    if member & 1:
        player = player ^ masks[0]
    if member & 2:
        player = player ^ masks[1]
    return player


def role_of(device, masks):
    low = jnp.where((device & masks[0]) != 0, 1, 0)
    high = jnp.where((device & masks[1]) != 0, 2, 0)
    return low + high


def masks_of(partners_ref):
    first, second = partners_ref[0, 0], partners_ref[1, 0]
    return jnp.minimum(first, second), jnp.maximum(first, second)


def pack_kernel(me_ref, partners_ref, start_hbm, source_hbm, out_hbm, pair_ref, *scratch):
    source, wide, staged, start, got, sent, start_got = scratch
    parts, capacity, quarter = source.shape
    tiles = quarter // LANES
    takers = staged.shape[1]
    start_rows = start.shape[0]
    low, high = masks_of(partners_ref)
    row = me_ref[0] % start_rows

    def load(part):
        return pltpu.make_async_copy(
            source_hbm.at[:, pl.ds(part * quarter, quarter)], source.at[part], got.at[part]
        )

    start_load = pltpu.make_async_copy(
        start_hbm.at[pl.ds(pl.multiple_of(me_ref[0] - row, start_rows), start_rows)], start, start_got
    )
    start_load.start()
    for part in range(parts):
        load(part).start()
    pair_ref[0] = pair_index(low, high, (out_hbm.shape[0] - 1).bit_length())
    start_load.wait()

    def one_part(part, carry):
        role_bits = jnp.where((part & 1) != 0, low, 0) | jnp.where((part & 2) != 0, high, 0)

        def taker(at):
            spread = (at & (low - 1)) | ((at & ~(low - 1)) << 1)
            return (spread & (high - 1)) | ((spread & ~(high - 1)) << 1) | role_bits

        def fill(at, carry):
            device = taker(at)
            for member in range(MEMBERS):
                begin = start[row, relative_player(device, member, (low, high))]
                rows = [wide[tile, pl.ds(begin, SLOT), :] for tile in range(tiles)]
                staged[part, at, pl.ds(member * SLOT, SLOT), :] = jnp.concatenate(rows, axis=1).astype(jnp.bfloat16)
            return carry

        def send(at, carry):
            pltpu.make_async_copy(staged.at[part, at], out_hbm.at[taker(at)], sent.at[part]).start()
            return carry

        load(part).wait()
        for tile in range(tiles):
            wide[tile] = source[part, :, pl.ds(tile * LANES, LANES)].astype(jnp.float32)
        for half in range(2):
            begin, end = half * takers // 2, (half + 1) * takers // 2
            lax.fori_loop(begin, end, fill, 0, unroll=4)
            lax.fori_loop(begin, end, send, 0, unroll=4)
        return carry

    lax.fori_loop(0, parts, one_part, 0)
    for part in range(parts):
        pltpu.make_async_copy(staged.at[part], out_hbm.at[pl.ds(0, takers)], sent.at[part]).wait()


def pair_index(low, high, bits):
    low_bit = sum(jnp.where(low >= 1 << at, 1, 0) for at in range(1, bits))
    high_bit = sum(jnp.where(high >= 1 << at, 1, 0) for at in range(1, bits))
    return (low_bit * (2 * bits - 1 - low_bit)) // 2 + high_bit - low_bit - 1


def pack(source_rows, me, partners, plan_start):
    capacity, feats = source_rows.shape
    devices = plan_start.shape[0]
    quarter = feats // MEMBERS
    smem, anywhere = pl.BlockSpec(memory_space=pltpu.SMEM), pl.BlockSpec(memory_space=pl.ANY)
    return pl.pallas_call(
        pack_kernel,
        in_specs=[smem, smem, anywhere, anywhere],
        out_specs=[anywhere, smem],
        scratch_shapes=[
            pltpu.VMEM((MEMBERS, capacity, quarter), jnp.bfloat16),
            pltpu.VMEM((quarter // LANES, capacity, LANES), jnp.float32),
            pltpu.VMEM((MEMBERS, devices // MEMBERS, MEMBERS * SLOT, quarter), jnp.bfloat16),
            pltpu.SMEM((8, devices), jnp.int32),
            pltpu.SemaphoreType.DMA((MEMBERS,)),
            pltpu.SemaphoreType.DMA((MEMBERS,)),
            pltpu.SemaphoreType.DMA,
        ],
        out_shape=[
            jax.ShapeDtypeStruct((devices, MEMBERS * SLOT, quarter), jnp.bfloat16),
            jax.ShapeDtypeStruct((1,), jnp.int32),
        ],
        compiler_params=pltpu.CompilerParams(vmem_limit_bytes=56 * 1024 * 1024),
        name="pack",
    )(me, partners, plan_start, source_rows)


def partial_kernel(scale, me_ref, partners_ref, count_hbm, received_hbm, factor_hbm, *refs):
    own, *out_hbm = refs[:3]
    received, factor, wide, conditioned, lent, count, got, loaded, sent = refs[3:]
    groups, group, _, quarter = received.shape
    tiles = quarter // LANES
    rows = wide.shape[2] - SLOT
    layers, width, _ = factor.shape
    each = width // LANES
    masks = masks_of(partners_ref)
    players = [relative_player(me_ref[0], member, masks) for member in range(MEMBERS)]

    def load(at):
        return pltpu.make_async_copy(received_hbm.at[pl.ds(at * group, group)], received.at[at], got.at[at])

    count_load = pltpu.make_async_copy(count_hbm, count, loaded.at[0])
    factor_load = pltpu.make_async_copy(
        factor_hbm.at[pl.ds(role_of(me_ref[0], masks) * layers, layers)], factor, loaded.at[1]
    )
    count_load.start()
    for at in range(groups):
        load(at).start()
    factor_load.start()
    count_load.wait()

    def one_group(at, begins):
        def one_source(source, begins):
            later = []
            for member in range(MEMBERS):
                run = received[at, source, pl.ds(member * SLOT, SLOT), :].astype(jnp.float32)
                for tile in range(tiles):
                    wide[member, tile, pl.ds(begins[member], SLOT), :] = run[:, tile * LANES : (tile + 1) * LANES]
                later.append(begins[member] + count[at * group + source, players[member]])
            return tuple(later)

        load(at).wait()
        return lax.fori_loop(0, group, one_source, begins, unroll=4)

    lax.fori_loop(0, groups, one_group, (jnp.int32(0),) * MEMBERS)
    factor_load.wait()
    for member in range(MEMBERS):
        for layer in range(layers):
            ordered = jnp.concatenate(
                [
                    wide[member, layer * each + tile, pl.ds(0, rows), :].astype(jnp.bfloat16)
                    for tile in range(each)
                ],
                axis=1,
            )
            conditioned[member, :, pl.ds(layer * width, width)] = jnp.dot(
                ordered, factor[layer], preferred_element_type=jnp.float32
            ).astype(jnp.bfloat16)

    def tile_of(left, right):
        return scale * lax.dot_general(
            conditioned[left],
            conditioned[right],
            (((1,), (1,)), ((), ())),
            preferred_element_type=jnp.float32,
        )

    copies = [pltpu.make_async_copy(lent.at[at], out_hbm[at], sent.at[at]) for at in range(2)]
    lent[0] = tile_of(1, 3).astype(jnp.bfloat16)
    turn = jnp.where(shares_ring(*masks), 1, 0)
    lent[1] = tile_of(2 + turn, 3 - turn).astype(jnp.bfloat16)
    copies[0].start()
    own[0] = tile_of(0, 1)
    copies[1].start()
    own[1] = tile_of(0, 2)
    for copy in copies:
        copy.wait()


def partial_tiles(received, factor, me, partners, plan_count, scale):
    devices, slots, quarter = received.shape
    width = factor.shape[1]
    layers = quarter // width
    rows = devices * SLOT // 2
    groups = 8
    smem, anywhere = pl.BlockSpec(memory_space=pltpu.SMEM), pl.BlockSpec(memory_space=pl.ANY)
    return pl.pallas_call(
        functools.partial(partial_kernel, scale),
        in_specs=[smem, smem, anywhere, anywhere, anywhere],
        out_specs=[pl.BlockSpec(memory_space=pltpu.VMEM), anywhere, anywhere],
        scratch_shapes=[
            pltpu.VMEM((groups, devices // groups, slots, quarter), jnp.bfloat16),
            pltpu.VMEM((layers, width, width), jnp.bfloat16),
            pltpu.VMEM((MEMBERS, quarter // LANES, rows + SLOT, LANES), jnp.float32),
            pltpu.VMEM((MEMBERS, rows, quarter), jnp.bfloat16),
            pltpu.VMEM((2, rows, rows), jnp.bfloat16),
            pltpu.SMEM((devices, devices), jnp.int32),
            pltpu.SemaphoreType.DMA((groups,)),
            pltpu.SemaphoreType.DMA((2,)),
            pltpu.SemaphoreType.DMA((2,)),
        ],
        out_shape=[
            pltpu.VMEM((2, rows, rows), jnp.float32),
            jax.ShapeDtypeStruct((rows, rows), jnp.bfloat16),
            jax.ShapeDtypeStruct((rows, rows), jnp.bfloat16),
        ],
        compiler_params=pltpu.CompilerParams(vmem_limit_bytes=40 * 1024 * 1024),
        name="partial_tiles",
    )(me, partners, plan_count, received, factor)


def half_sums_kernel(own, *refs):
    added_hbm, out_hbm, (added, half, got, sent) = refs[:2], refs[2:4], refs[4:]
    loads = [pltpu.make_async_copy(added_hbm[at], added.at[at], got.at[at]) for at in range(2)]
    sends = [pltpu.make_async_copy(half.at[at], out_hbm[at], sent.at[at]) for at in range(2)]
    for load in loads:
        load.start()
    for at in range(2):
        loads[at].wait()
        half[at] = (own[at] + added[at].astype(jnp.float32)).astype(jnp.bfloat16)
        sends[at].start()
    for send in sends:
        send.wait()


def half_sums(own, first, second):
    rows = own.shape[1]
    anywhere, vmem = pl.BlockSpec(memory_space=pl.ANY), pl.BlockSpec(memory_space=pltpu.VMEM)
    return pl.pallas_call(
        half_sums_kernel,
        in_specs=[vmem, anywhere, anywhere],
        out_specs=[anywhere, anywhere],
        scratch_shapes=[
            pltpu.VMEM((2, rows, rows), jnp.bfloat16),
            pltpu.VMEM((2, rows, rows), jnp.bfloat16),
            pltpu.SemaphoreType.DMA((2,)),
            pltpu.SemaphoreType.DMA((2,)),
        ],
        out_shape=[jax.ShapeDtypeStruct((rows, rows), jnp.bfloat16)] * 2,
        compiler_params=pltpu.CompilerParams(vmem_limit_bytes=16 * 1024 * 1024),
        name="half_sums",
    )(pltpu.with_memory_space_constraint(own, pltpu.VMEM), first, second)


def finish_kernel(partners_ref, own, *refs):
    added_hbm, turned_hbm, out_hbm, (added, turned, tile, got, sent) = refs[:2], refs[2:4], refs[4], refs[5:]
    swapped = jnp.where(partners_ref[0, 0] < partners_ref[1, 0], 0, 1)
    loads = [
        [
            pltpu.make_async_copy(added_hbm[at], added.at[at], got.at[2 * at]),
            pltpu.make_async_copy(turned_hbm[at], turned.at[at], got.at[2 * at + 1]),
        ]
        for at in range(2)
    ]
    sends = [pltpu.make_async_copy(tile.at[at], out_hbm.at[at ^ swapped], sent.at[at]) for at in range(2)]
    for load in loads[0] + loads[1]:
        load.start()
    for at in range(2):
        for load in loads[at]:
            load.wait()
        tile[at] = own[at] + added[at].astype(jnp.float32) + turned[at].astype(jnp.float32).T
        sends[at].start()
    for send in sends:
        send.wait()


def finish(partners, own, added, turned):
    rows = own.shape[1]
    smem, anywhere = pl.BlockSpec(memory_space=pltpu.SMEM), pl.BlockSpec(memory_space=pl.ANY)
    return pl.pallas_call(
        finish_kernel,
        in_specs=[smem, pl.BlockSpec(memory_space=pltpu.VMEM), *[anywhere] * 4],
        out_specs=anywhere,
        scratch_shapes=[
            pltpu.VMEM((2, rows, rows), jnp.bfloat16),
            pltpu.VMEM((2, rows, rows), jnp.bfloat16),
            pltpu.VMEM((2, rows, rows), jnp.float32),
            pltpu.SemaphoreType.DMA((4,)),
            pltpu.SemaphoreType.DMA((2,)),
        ],
        out_shape=jax.ShapeDtypeStruct((2, rows, rows), jnp.float32),
        compiler_params=pltpu.CompilerParams(vmem_limit_bytes=16 * 1024 * 1024),
        name="finish",
    )(partners, pltpu.with_memory_space_constraint(own, pltpu.VMEM), *added, *turned)


def exchange(pair, devices, bits, over_low, over_high, first):
    def branch(low, high):
        if first and shares_ring(low, high):
            high = low ^ high

        def swap(a, b):
            return (
                lax.ppermute(a, "dev", [(at, at ^ low) for at in range(devices)]),
                lax.ppermute(b, "dev", [(at, at ^ high) for at in range(devices)]),
            )

        return swap

    branches = [branch(1 << low, 1 << high) for low in range(bits) for high in range(low + 1, bits)]
    return lax.switch(pair, branches, over_low, over_high)


def per_device(source_rows, factor, plan_start, plan_count, partners):
    devices = lax.axis_size("dev")
    bits = devices.bit_length() - 1
    me = lax.axis_index("dev").reshape(1)
    packed, pair = pack(source_rows, me, partners, plan_start)
    received = lax.all_to_all(packed, "dev", split_axis=0, concat_axis=0, tiled=True)
    received, pair = lax.optimization_barrier((received, pair))
    own, for_low, for_high = partial_tiles(received, factor, me, partners, plan_count, source_rows.shape[1] ** -0.5)
    from_low, from_high = exchange(pair[0], devices, bits, for_low, for_high, True)
    halves = half_sums(own, from_high, from_low)
    return finish(partners, own, (from_high, from_low), exchange(pair[0], devices, bits, *halves, False))


def solution(mesh):
    placed = (P("dev", None), P(), P(), P(), P())
    return jax.shard_map(
        per_device, mesh=mesh, in_specs=placed, out_specs=P(None, "dev", None), check_vma=False
    )
```

```python
import functools

import jax
import jax.numpy as jnp
from jax import lax
from jax.experimental import pallas as pl
from jax.experimental.pallas import tpu as pltpu
from jax.sharding import PartitionSpec as P

SLOT = 8
LANES = 128
MEMBERS = 4
RING_BITS = 0b0101010


def shares_ring(low, high):
    return ((low & RING_BITS) != 0) & (high == 2 * low)


def relative_player(device, member, masks):
    player = device
    if member & 1:
        player = player ^ masks[0]
    if member & 2:
        player = player ^ masks[1]
    return player


def role_of(device, masks):
    low = jnp.where((device & masks[0]) != 0, 1, 0)
    high = jnp.where((device & masks[1]) != 0, 2, 0)
    return low + high


def masks_of(partners_ref):
    first, second = partners_ref[0, 0], partners_ref[1, 0]
    return jnp.minimum(first, second), jnp.maximum(first, second)


def pack_kernel(me_ref, partners_ref, start_hbm, source_hbm, out_ref, pair_ref, *scratch):
    source, wide, start, got, start_got = scratch
    parts, capacity, quarter = source.shape
    tiles = quarter // LANES
    takers = out_ref.shape[0] // parts
    start_rows = start.shape[0]
    low, high = masks_of(partners_ref)
    row = me_ref[0] % start_rows

    def load(part):
        return pltpu.make_async_copy(
            source_hbm.at[:, pl.ds(part * quarter, quarter)], source.at[part], got.at[part]
        )

    start_load = pltpu.make_async_copy(
        start_hbm.at[pl.ds(pl.multiple_of(me_ref[0] - row, start_rows), start_rows)], start, start_got
    )
    start_load.start()
    for part in range(parts):
        load(part).start()
    pair_ref[0] = pair_index(low, high, (out_ref.shape[0] - 1).bit_length())
    start_load.wait()

    def one_part(part, carry):
        role_bits = jnp.where((part & 1) != 0, low, 0) | jnp.where((part & 2) != 0, high, 0)

        def taker(at):
            spread = (at & (low - 1)) | ((at & ~(low - 1)) << 1)
            return (spread & (high - 1)) | ((spread & ~(high - 1)) << 1) | role_bits

        def fill(at, carry):
            device = taker(at)
            for member in range(MEMBERS):
                begin = start[row, relative_player(device, member, (low, high))]
                rows = [wide[tile, pl.ds(begin, SLOT), :] for tile in range(tiles)]
                out_ref[device, pl.ds(member * SLOT, SLOT), :] = jnp.concatenate(rows, axis=1).astype(jnp.bfloat16)
            return carry

        load(part).wait()
        for tile in range(tiles):
            wide[tile] = source[part, :, pl.ds(tile * LANES, LANES)].astype(jnp.float32)
        return lax.fori_loop(0, takers, fill, carry, unroll=8)

    lax.fori_loop(0, parts, one_part, 0)


def pair_index(low, high, bits):
    low_bit = sum(jnp.where(low >= 1 << at, 1, 0) for at in range(1, bits))
    high_bit = sum(jnp.where(high >= 1 << at, 1, 0) for at in range(1, bits))
    return (low_bit * (2 * bits - 1 - low_bit)) // 2 + high_bit - low_bit - 1


def pack(source_rows, me, partners, plan_start):
    capacity, feats = source_rows.shape
    devices = plan_start.shape[0]
    quarter = feats // MEMBERS
    smem, anywhere = pl.BlockSpec(memory_space=pltpu.SMEM), pl.BlockSpec(memory_space=pl.ANY)
    return pl.pallas_call(
        pack_kernel,
        in_specs=[smem, smem, anywhere, anywhere],
        out_specs=[pl.BlockSpec(memory_space=pltpu.VMEM), smem],
        scratch_shapes=[
            pltpu.VMEM((MEMBERS, capacity, quarter), jnp.bfloat16),
            pltpu.VMEM((quarter // LANES, capacity, LANES), jnp.float32),
            pltpu.SMEM((8, devices), jnp.int32),
            pltpu.SemaphoreType.DMA((MEMBERS,)),
            pltpu.SemaphoreType.DMA,
        ],
        out_shape=[
            pltpu.VMEM((devices, MEMBERS * SLOT, quarter), jnp.bfloat16),
            jax.ShapeDtypeStruct((1,), jnp.int32),
        ],
        compiler_params=pltpu.CompilerParams(vmem_limit_bytes=52 * 1024 * 1024),
        name="pack",
    )(me, partners, plan_start, source_rows)


def partial_kernel(scale, me_ref, partners_ref, count_hbm, received_hbm, factor_hbm, *refs):
    own, *out_hbm = refs[:3]
    received, factor, wide, conditioned, lent, count, got, loaded, sent = refs[3:]
    groups, group, _, quarter = received.shape
    tiles = quarter // LANES
    rows = wide.shape[2] - SLOT
    layers, width, _ = factor.shape
    each = width // LANES
    masks = masks_of(partners_ref)
    players = [relative_player(me_ref[0], member, masks) for member in range(MEMBERS)]

    def load(at):
        return pltpu.make_async_copy(received_hbm.at[pl.ds(at * group, group)], received.at[at], got.at[at])

    count_load = pltpu.make_async_copy(count_hbm, count, loaded.at[0])
    factor_load = pltpu.make_async_copy(
        factor_hbm.at[pl.ds(role_of(me_ref[0], masks) * layers, layers)], factor, loaded.at[1]
    )
    count_load.start()
    for at in range(groups):
        load(at).start()
    factor_load.start()
    count_load.wait()

    def one_group(at, begins):
        def one_source(source, begins):
            later = []
            for member in range(MEMBERS):
                run = received[at, source, pl.ds(member * SLOT, SLOT), :].astype(jnp.float32)
                for tile in range(tiles):
                    wide[member, tile, pl.ds(begins[member], SLOT), :] = run[:, tile * LANES : (tile + 1) * LANES]
                later.append(begins[member] + count[at * group + source, players[member]])
            return tuple(later)

        load(at).wait()
        return lax.fori_loop(0, group, one_source, begins, unroll=4)

    lax.fori_loop(0, groups, one_group, (jnp.int32(0),) * MEMBERS)
    factor_load.wait()
    for member in range(MEMBERS):
        for layer in range(layers):
            ordered = jnp.concatenate(
                [
                    wide[member, layer * each + tile, pl.ds(0, rows), :].astype(jnp.bfloat16)
                    for tile in range(each)
                ],
                axis=1,
            )
            conditioned[member, :, pl.ds(layer * width, width)] = jnp.dot(
                ordered, factor[layer], preferred_element_type=jnp.float32
            ).astype(jnp.bfloat16)

    def tile_of(left, right):
        return scale * lax.dot_general(
            conditioned[left],
            conditioned[right],
            (((1,), (1,)), ((), ())),
            preferred_element_type=jnp.float32,
        )

    copies = [pltpu.make_async_copy(lent.at[at], out_hbm[at], sent.at[at]) for at in range(2)]
    lent[0] = tile_of(1, 3).astype(jnp.bfloat16)
    turn = jnp.where(shares_ring(*masks), 1, 0)
    lent[1] = tile_of(2 + turn, 3 - turn).astype(jnp.bfloat16)
    copies[0].start()
    own[0] = tile_of(0, 1)
    copies[1].start()
    own[1] = tile_of(0, 2)
    for copy in copies:
        copy.wait()


def partial_tiles(received, factor, me, partners, plan_count, scale):
    devices, slots, quarter = received.shape
    width = factor.shape[1]
    layers = quarter // width
    rows = devices * SLOT // 2
    groups = 8
    smem, anywhere = pl.BlockSpec(memory_space=pltpu.SMEM), pl.BlockSpec(memory_space=pl.ANY)
    return pl.pallas_call(
        functools.partial(partial_kernel, scale),
        in_specs=[smem, smem, anywhere, anywhere, anywhere],
        out_specs=[pl.BlockSpec(memory_space=pltpu.VMEM), anywhere, anywhere],
        scratch_shapes=[
            pltpu.VMEM((groups, devices // groups, slots, quarter), jnp.bfloat16),
            pltpu.VMEM((layers, width, width), jnp.bfloat16),
            pltpu.VMEM((MEMBERS, quarter // LANES, rows + SLOT, LANES), jnp.float32),
            pltpu.VMEM((MEMBERS, rows, quarter), jnp.bfloat16),
            pltpu.VMEM((2, rows, rows), jnp.bfloat16),
            pltpu.SMEM((devices, devices), jnp.int32),
            pltpu.SemaphoreType.DMA((groups,)),
            pltpu.SemaphoreType.DMA((2,)),
            pltpu.SemaphoreType.DMA((2,)),
        ],
        out_shape=[
            pltpu.VMEM((2, rows, rows), jnp.float32),
            jax.ShapeDtypeStruct((rows, rows), jnp.bfloat16),
            jax.ShapeDtypeStruct((rows, rows), jnp.bfloat16),
        ],
        compiler_params=pltpu.CompilerParams(vmem_limit_bytes=40 * 1024 * 1024),
        name="partial_tiles",
    )(me, partners, plan_count, received, factor)


def half_sums_kernel(own, *refs):
    added_hbm, out_hbm, (added, half, got, sent) = refs[:2], refs[2:4], refs[4:]
    loads = [pltpu.make_async_copy(added_hbm[at], added.at[at], got.at[at]) for at in range(2)]
    sends = [pltpu.make_async_copy(half.at[at], out_hbm[at], sent.at[at]) for at in range(2)]
    for load in loads:
        load.start()
    for at in range(2):
        loads[at].wait()
        half[at] = (own[at] + added[at].astype(jnp.float32)).astype(jnp.bfloat16)
        sends[at].start()
    for send in sends:
        send.wait()


def half_sums(own, first, second):
    rows = own.shape[1]
    anywhere, vmem = pl.BlockSpec(memory_space=pl.ANY), pl.BlockSpec(memory_space=pltpu.VMEM)
    return pl.pallas_call(
        half_sums_kernel,
        in_specs=[vmem, anywhere, anywhere],
        out_specs=[anywhere, anywhere],
        scratch_shapes=[
            pltpu.VMEM((2, rows, rows), jnp.bfloat16),
            pltpu.VMEM((2, rows, rows), jnp.bfloat16),
            pltpu.SemaphoreType.DMA((2,)),
            pltpu.SemaphoreType.DMA((2,)),
        ],
        out_shape=[jax.ShapeDtypeStruct((rows, rows), jnp.bfloat16)] * 2,
        compiler_params=pltpu.CompilerParams(vmem_limit_bytes=16 * 1024 * 1024),
        name="half_sums",
    )(pltpu.with_memory_space_constraint(own, pltpu.VMEM), first, second)


def finish_kernel(partners_ref, own, *refs):
    added_hbm, turned_hbm, out_hbm, (added, turned, tile, got, sent) = refs[:2], refs[2:4], refs[4], refs[5:]
    swapped = jnp.where(partners_ref[0, 0] < partners_ref[1, 0], 0, 1)
    loads = [
        [
            pltpu.make_async_copy(added_hbm[at], added.at[at], got.at[2 * at]),
            pltpu.make_async_copy(turned_hbm[at], turned.at[at], got.at[2 * at + 1]),
        ]
        for at in range(2)
    ]
    sends = [pltpu.make_async_copy(tile.at[at], out_hbm.at[at ^ swapped], sent.at[at]) for at in range(2)]
    for load in loads[0] + loads[1]:
        load.start()
    for at in range(2):
        for load in loads[at]:
            load.wait()
        tile[at] = own[at] + added[at].astype(jnp.float32) + turned[at].astype(jnp.float32).T
        sends[at].start()
    for send in sends:
        send.wait()


def finish(partners, own, added, turned):
    rows = own.shape[1]
    smem, anywhere = pl.BlockSpec(memory_space=pltpu.SMEM), pl.BlockSpec(memory_space=pl.ANY)
    return pl.pallas_call(
        finish_kernel,
        in_specs=[smem, pl.BlockSpec(memory_space=pltpu.VMEM), *[anywhere] * 4],
        out_specs=anywhere,
        scratch_shapes=[
            pltpu.VMEM((2, rows, rows), jnp.bfloat16),
            pltpu.VMEM((2, rows, rows), jnp.bfloat16),
            pltpu.VMEM((2, rows, rows), jnp.float32),
            pltpu.SemaphoreType.DMA((4,)),
            pltpu.SemaphoreType.DMA((2,)),
        ],
        out_shape=jax.ShapeDtypeStruct((2, rows, rows), jnp.float32),
        compiler_params=pltpu.CompilerParams(vmem_limit_bytes=16 * 1024 * 1024),
        name="finish",
    )(partners, pltpu.with_memory_space_constraint(own, pltpu.VMEM), *added, *turned)


def exchange(pair, devices, bits, over_low, over_high, first):
    def branch(low, high):
        if first and shares_ring(low, high):
            high = low ^ high

        def swap(a, b):
            return (
                lax.ppermute(a, "dev", [(at, at ^ low) for at in range(devices)]),
                lax.ppermute(b, "dev", [(at, at ^ high) for at in range(devices)]),
            )

        return swap

    branches = [branch(1 << low, 1 << high) for low in range(bits) for high in range(low + 1, bits)]
    return lax.switch(pair, branches, over_low, over_high)


def per_device(source_rows, factor, plan_start, plan_count, partners):
    devices = lax.axis_size("dev")
    bits = devices.bit_length() - 1
    me = lax.axis_index("dev").reshape(1)
    packed, pair = pack(source_rows, me, partners, plan_start)
    received = lax.all_to_all(packed, "dev", split_axis=0, concat_axis=0, tiled=True)
    received, pair = lax.optimization_barrier((received, pair))
    own, for_low, for_high = partial_tiles(received, factor, me, partners, plan_count, source_rows.shape[1] ** -0.5)
    from_low, from_high = exchange(pair[0], devices, bits, for_low, for_high, True)
    halves = half_sums(own, from_high, from_low)
    return finish(partners, own, (from_high, from_low), exchange(pair[0], devices, bits, *halves, False))


def solution(mesh):
    placed = (P("dev", None), P(), P(), P(), P())
    return jax.shard_map(
        per_device, mesh=mesh, in_specs=placed, out_specs=P(None, "dev", None), check_vma=False
    )
```

```python
import functools

import jax
import jax.numpy as jnp
from jax import lax
from jax.experimental import pallas as pl
from jax.experimental.pallas import tpu as pltpu
from jax.sharding import PartitionSpec as P

SLOT = 8
LANES = 128
MEMBERS = 4
RING_BITS = 0b0101010


def shares_ring(low, high):
    return ((low & RING_BITS) != 0) & (high == 2 * low)


def relative_player(device, member, masks):
    player = device
    if member & 1:
        player = player ^ masks[0]
    if member & 2:
        player = player ^ masks[1]
    return player


def role_of(device, masks):
    low = jnp.where((device & masks[0]) != 0, 1, 0)
    high = jnp.where((device & masks[1]) != 0, 2, 0)
    return low + high


def masks_of(partners_ref):
    first, second = partners_ref[0, 0], partners_ref[1, 0]
    return jnp.minimum(first, second), jnp.maximum(first, second)


def pack_kernel(me_ref, partners_ref, start_hbm, source_hbm, out_ref, pair_ref, *scratch):
    source, wide, start, got, start_got = scratch
    parts, capacity, quarter = source.shape
    tiles = quarter // LANES
    takers = out_ref.shape[0] // parts
    start_rows = start.shape[0]
    low, high = masks_of(partners_ref)
    row = me_ref[0] % start_rows

    def load(part, half):
        width = quarter // 2
        return pltpu.make_async_copy(
            source_hbm.at[:, pl.ds(pl.multiple_of(part * quarter + half * width, width), width)],
            source.at[part, :, pl.ds(half * width, width)],
            got.at[part, half],
        )

    start_load = pltpu.make_async_copy(
        start_hbm.at[pl.ds(pl.multiple_of(me_ref[0] - row, start_rows), start_rows)], start, start_got
    )
    start_load.start()
    for part in range(parts):
        for half in range(2):
            load(part, half).start()
    pair_ref[0] = pair_index(low, high, (out_ref.shape[0] - 1).bit_length())
    start_load.wait()

    def one_part(part, carry):
        role_bits = jnp.where((part & 1) != 0, low, 0) | jnp.where((part & 2) != 0, high, 0)

        def taker(at):
            spread = (at & (low - 1)) | ((at & ~(low - 1)) << 1)
            return (spread & (high - 1)) | ((spread & ~(high - 1)) << 1) | role_bits

        def fill(at, carry):
            device = taker(at)
            for member in range(MEMBERS):
                begin = start[row, relative_player(device, member, (low, high))]
                rows = [wide[tile, pl.ds(begin, SLOT), :] for tile in range(tiles)]
                out_ref[device, pl.ds(member * SLOT, SLOT), :] = jnp.concatenate(rows, axis=1).astype(jnp.bfloat16)
            return carry

        for tile in range(tiles):
            if tile % (tiles // 2) == 0:
                load(part, tile // (tiles // 2)).wait()
            wide[tile] = source[part, :, pl.ds(tile * LANES, LANES)].astype(jnp.float32)
        return lax.fori_loop(0, takers, fill, carry, unroll=8)

    lax.fori_loop(0, parts, one_part, 0)


def pair_index(low, high, bits):
    low_bit = sum(jnp.where(low >= 1 << at, 1, 0) for at in range(1, bits))
    high_bit = sum(jnp.where(high >= 1 << at, 1, 0) for at in range(1, bits))
    return (low_bit * (2 * bits - 1 - low_bit)) // 2 + high_bit - low_bit - 1


def pack(source_rows, me, partners, plan_start):
    capacity, feats = source_rows.shape
    devices = plan_start.shape[0]
    quarter = feats // MEMBERS
    smem, anywhere = pl.BlockSpec(memory_space=pltpu.SMEM), pl.BlockSpec(memory_space=pl.ANY)
    return pl.pallas_call(
        pack_kernel,
        in_specs=[smem, smem, anywhere, anywhere],
        out_specs=[pl.BlockSpec(memory_space=pltpu.VMEM), smem],
        scratch_shapes=[
            pltpu.VMEM((MEMBERS, capacity, quarter), jnp.bfloat16),
            pltpu.VMEM((quarter // LANES, capacity, LANES), jnp.float32),
            pltpu.SMEM((8, devices), jnp.int32),
            pltpu.SemaphoreType.DMA((MEMBERS, 2)),
            pltpu.SemaphoreType.DMA,
        ],
        out_shape=[
            pltpu.VMEM((devices, MEMBERS * SLOT, quarter), jnp.bfloat16),
            jax.ShapeDtypeStruct((1,), jnp.int32),
        ],
        compiler_params=pltpu.CompilerParams(vmem_limit_bytes=52 * 1024 * 1024),
        name="pack",
    )(me, partners, plan_start, source_rows)


def partial_kernel(scale, me_ref, partners_ref, count_hbm, received_hbm, factor_hbm, *refs):
    own, *out_hbm = refs[:3]
    received, factor, wide, conditioned, lent, count, got, loaded, sent = refs[3:]
    groups, group, _, quarter = received.shape
    tiles = quarter // LANES
    rows = wide.shape[2] - SLOT
    layers, width, _ = factor.shape
    each = width // LANES
    masks = masks_of(partners_ref)
    players = [relative_player(me_ref[0], member, masks) for member in range(MEMBERS)]

    def load(at):
        return pltpu.make_async_copy(received_hbm.at[pl.ds(at * group, group)], received.at[at], got.at[at])

    count_load = pltpu.make_async_copy(count_hbm, count, loaded.at[0])
    factor_load = pltpu.make_async_copy(
        factor_hbm.at[pl.ds(role_of(me_ref[0], masks) * layers, layers)], factor, loaded.at[1]
    )
    count_load.start()
    for at in range(groups):
        load(at).start()
    factor_load.start()
    count_load.wait()

    def one_group(at, begins):
        def one_source(source, begins):
            later = []
            for member in range(MEMBERS):
                run = received[at, source, pl.ds(member * SLOT, SLOT), :].astype(jnp.float32)
                for tile in range(tiles):
                    wide[member, tile, pl.ds(begins[member], SLOT), :] = run[:, tile * LANES : (tile + 1) * LANES]
                later.append(begins[member] + count[at * group + source, players[member]])
            return tuple(later)

        load(at).wait()
        return lax.fori_loop(0, group, one_source, begins, unroll=4)

    lax.fori_loop(0, groups, one_group, (jnp.int32(0),) * MEMBERS)
    factor_load.wait()
    for member in range(MEMBERS):
        for layer in range(layers):
            ordered = jnp.concatenate(
                [
                    wide[member, layer * each + tile, pl.ds(0, rows), :].astype(jnp.bfloat16)
                    for tile in range(each)
                ],
                axis=1,
            )
            conditioned[member, :, pl.ds(layer * width, width)] = jnp.dot(
                ordered, factor[layer], preferred_element_type=jnp.float32
            ).astype(jnp.bfloat16)

    def tile_of(left, right):
        return scale * lax.dot_general(
            conditioned[left],
            conditioned[right],
            (((1,), (1,)), ((), ())),
            preferred_element_type=jnp.float32,
        )

    copies = [pltpu.make_async_copy(lent.at[at], out_hbm[at], sent.at[at]) for at in range(2)]
    lent[0] = tile_of(1, 3).astype(jnp.bfloat16)
    turn = jnp.where(shares_ring(*masks), 1, 0)
    lent[1] = tile_of(2 + turn, 3 - turn).astype(jnp.bfloat16)
    copies[0].start()
    own[0] = tile_of(0, 1)
    copies[1].start()
    own[1] = tile_of(0, 2)
    for copy in copies:
        copy.wait()


def partial_tiles(received, factor, me, partners, plan_count, scale):
    devices, slots, quarter = received.shape
    width = factor.shape[1]
    layers = quarter // width
    rows = devices * SLOT // 2
    groups = 8
    smem, anywhere = pl.BlockSpec(memory_space=pltpu.SMEM), pl.BlockSpec(memory_space=pl.ANY)
    return pl.pallas_call(
        functools.partial(partial_kernel, scale),
        in_specs=[smem, smem, anywhere, anywhere, anywhere],
        out_specs=[pl.BlockSpec(memory_space=pltpu.VMEM), anywhere, anywhere],
        scratch_shapes=[
            pltpu.VMEM((groups, devices // groups, slots, quarter), jnp.bfloat16),
            pltpu.VMEM((layers, width, width), jnp.bfloat16),
            pltpu.VMEM((MEMBERS, quarter // LANES, rows + SLOT, LANES), jnp.float32),
            pltpu.VMEM((MEMBERS, rows, quarter), jnp.bfloat16),
            pltpu.VMEM((2, rows, rows), jnp.bfloat16),
            pltpu.SMEM((devices, devices), jnp.int32),
            pltpu.SemaphoreType.DMA((groups,)),
            pltpu.SemaphoreType.DMA((2,)),
            pltpu.SemaphoreType.DMA((2,)),
        ],
        out_shape=[
            pltpu.VMEM((2, rows, rows), jnp.float32),
            jax.ShapeDtypeStruct((rows, rows), jnp.bfloat16),
            jax.ShapeDtypeStruct((rows, rows), jnp.bfloat16),
        ],
        compiler_params=pltpu.CompilerParams(vmem_limit_bytes=40 * 1024 * 1024),
        name="partial_tiles",
    )(me, partners, plan_count, received, factor)


def half_sums_kernel(own, *refs):
    added_hbm, out_hbm, (added, half, got, sent) = refs[:2], refs[2:4], refs[4:]
    loads = [pltpu.make_async_copy(added_hbm[at], added.at[at], got.at[at]) for at in range(2)]
    sends = [pltpu.make_async_copy(half.at[at], out_hbm[at], sent.at[at]) for at in range(2)]
    for load in loads:
        load.start()
    for at in range(2):
        loads[at].wait()
        half[at] = (own[at] + added[at].astype(jnp.float32)).astype(jnp.bfloat16)
        sends[at].start()
    for send in sends:
        send.wait()


def half_sums(own, first, second):
    rows = own.shape[1]
    anywhere, vmem = pl.BlockSpec(memory_space=pl.ANY), pl.BlockSpec(memory_space=pltpu.VMEM)
    return pl.pallas_call(
        half_sums_kernel,
        in_specs=[vmem, anywhere, anywhere],
        out_specs=[anywhere, anywhere],
        scratch_shapes=[
            pltpu.VMEM((2, rows, rows), jnp.bfloat16),
            pltpu.VMEM((2, rows, rows), jnp.bfloat16),
            pltpu.SemaphoreType.DMA((2,)),
            pltpu.SemaphoreType.DMA((2,)),
        ],
        out_shape=[jax.ShapeDtypeStruct((rows, rows), jnp.bfloat16)] * 2,
        compiler_params=pltpu.CompilerParams(vmem_limit_bytes=16 * 1024 * 1024),
        name="half_sums",
    )(pltpu.with_memory_space_constraint(own, pltpu.VMEM), first, second)


def finish_kernel(partners_ref, own, *refs):
    added_hbm, turned_hbm, out_hbm, (added, turned, tile, got, sent) = refs[:2], refs[2:4], refs[4], refs[5:]
    swapped = jnp.where(partners_ref[0, 0] < partners_ref[1, 0], 0, 1)
    loads = [
        [
            pltpu.make_async_copy(added_hbm[at], added.at[at], got.at[2 * at]),
            pltpu.make_async_copy(turned_hbm[at], turned.at[at], got.at[2 * at + 1]),
        ]
        for at in range(2)
    ]
    sends = [pltpu.make_async_copy(tile.at[at], out_hbm.at[at ^ swapped], sent.at[at]) for at in range(2)]
    for load in loads[0] + loads[1]:
        load.start()
    for at in range(2):
        for load in loads[at]:
            load.wait()
        tile[at] = own[at] + added[at].astype(jnp.float32) + turned[at].astype(jnp.float32).T
        sends[at].start()
    for send in sends:
        send.wait()


def finish(partners, own, added, turned):
    rows = own.shape[1]
    smem, anywhere = pl.BlockSpec(memory_space=pltpu.SMEM), pl.BlockSpec(memory_space=pl.ANY)
    return pl.pallas_call(
        finish_kernel,
        in_specs=[smem, pl.BlockSpec(memory_space=pltpu.VMEM), *[anywhere] * 4],
        out_specs=anywhere,
        scratch_shapes=[
            pltpu.VMEM((2, rows, rows), jnp.bfloat16),
            pltpu.VMEM((2, rows, rows), jnp.bfloat16),
            pltpu.VMEM((2, rows, rows), jnp.float32),
            pltpu.SemaphoreType.DMA((4,)),
            pltpu.SemaphoreType.DMA((2,)),
        ],
        out_shape=jax.ShapeDtypeStruct((2, rows, rows), jnp.float32),
        compiler_params=pltpu.CompilerParams(vmem_limit_bytes=16 * 1024 * 1024),
        name="finish",
    )(partners, pltpu.with_memory_space_constraint(own, pltpu.VMEM), *added, *turned)


def exchange(pair, devices, bits, over_low, over_high, first):
    def branch(low, high):
        if first and shares_ring(low, high):
            high = low ^ high

        def swap(a, b):
            return (
                lax.ppermute(a, "dev", [(at, at ^ low) for at in range(devices)]),
                lax.ppermute(b, "dev", [(at, at ^ high) for at in range(devices)]),
            )

        return swap

    branches = [branch(1 << low, 1 << high) for low in range(bits) for high in range(low + 1, bits)]
    return lax.switch(pair, branches, over_low, over_high)


def per_device(source_rows, factor, plan_start, plan_count, partners):
    devices = lax.axis_size("dev")
    bits = devices.bit_length() - 1
    me = lax.axis_index("dev").reshape(1)
    packed, pair = pack(source_rows, me, partners, plan_start)
    received = lax.all_to_all(packed, "dev", split_axis=0, concat_axis=0, tiled=True)
    received, pair = lax.optimization_barrier((received, pair))
    own, for_low, for_high = partial_tiles(received, factor, me, partners, plan_count, source_rows.shape[1] ** -0.5)
    from_low, from_high = exchange(pair[0], devices, bits, for_low, for_high, True)
    halves = half_sums(own, from_high, from_low)
    return finish(partners, own, (from_high, from_low), exchange(pair[0], devices, bits, *halves, False))


def solution(mesh):
    placed = (P("dev", None), P(), P(), P(), P())
    return jax.shard_map(
        per_device, mesh=mesh, in_specs=placed, out_specs=P(None, "dev", None), check_vma=False
    )
```
